128 devices in a mesh: row: 8 (over x, y_hi), col: 16 (over z, y_lo, core).
Axes of the slice: x: 4, y: 4 (y_hi: 2, y_lo: 2; y = y_hi * 2 + y_lo), z: 4, core: 2. Of those that a mesh axis runs over, the one named last changes fastest.
Arguments:
- latent: bfloat16 [128, 128, 256], P('row', 'col'), may hold values from -6 to 6
- well_logs: bfloat16 [128, 256], P(('row', 'col')), may hold values from -6 to 6
- cond_weight: bfloat16 [256, 256], replicated, may hold values from -0.375 to 0.375
- trace_rows: int32 [128], P('col'), may hold values from 0 to 127, as said below
- norm_gain: float32 [256], replicated, may hold values from 0.5 to 1.5
- in_weight: bfloat16 [256, 512], replicated, may hold values from -0.375 to 0.375
- conv_weight: float32 [9, 256], replicated, may hold values from -2 to 2
- bc_weight: bfloat16 [256, 1024], replicated, may hold values from -0.375 to 0.375
- dt_weight: bfloat16 [256, 64], replicated, may hold values from -0.375 to 0.375
- dt_bias: float32 [4, 16], replicated, may hold values from -0.5 to 0.5
- row_rate: float32 [2, 16], replicated, may hold values from 1 to 512
- col_rate: float32 [2, 16], replicated, may hold values from 1 to 512
- horizon: float32 [128, 128], P('row', 'col'), may hold values from 0 to 1
- out_gain: float32 [256], replicated, may hold values from 0.5 to 1.5
- out_weight: bfloat16 [256, 256], replicated, may hold values from -0.375 to 0.375
Outputs:
- block_out: bfloat16 [128, 128, 256], P('row', 'col')
The draws below stay inside these ranges and needn't reach their ends.
Inputs may be any that keep to these rules, and one draw needn't show every extreme that they name: `trace_rows`: every conditioning token row is named by some plane column.
All inputs are finite; a program needn't handle non-finite values.
Results may differ from the reference program's by a relative error of at most 0.009.
Values may be sent and summed in bfloat16 or wider, within the bound.
No kernel may reach another device: no remote copies, remote signals or barrier semaphores. Data moves between devices by JAX's collectives and lax.ppermute only.
A program may use at most 192 MiB of HBM per device.

```python
import math
import jax
import jax.numpy as jnp
from jax import lax

D = 256
E = 256
HEADS = 16
STATE = 128
HEAD_DIM = 16
GRID_ROW_COUNT = 128
GRID_COLUMN_COUNT = 128
NCOND = 128


def draw_trace_rows(key, part):
    order = jax.random.permutation(key, GRID_COLUMN_COUNT)
    return (order * NCOND // GRID_COLUMN_COUNT).astype(jnp.int32)


def rate_table(key):
    key_slow = jax.random.fold_in(key, 0)
    values = jnp.exp(jax.random.uniform(key_slow, (2 * HEADS,), jnp.float32, math.log(1.0), math.log(512.0)))
    return values.reshape(2, HEADS).astype(jnp.float32)


def draw_row_rate(key, part):
    return rate_table(jax.random.fold_in(key, 11))


def draw_col_rate(key, part):
    return rate_table(jax.random.fold_in(key, 23))


def draw_horizon(key, part):
    random_seed_offset, key_spike, key_root = jax.random.split(key, 3)
    sudden_jumps = jax.random.uniform(random_seed_offset, (GRID_ROW_COUNT, GRID_COLUMN_COUNT), jnp.float32) < 1.0 / 512.0
    large_amplitude_trace = jax.random.uniform(key_spike, (GRID_ROW_COUNT, GRID_COLUMN_COUNT), jnp.float32, 0.22, 0.7)
    faint_amplitude_trace = jax.random.uniform(key_root, (GRID_ROW_COUNT, GRID_COLUMN_COUNT), jnp.float32, 0.0, 0.002)
    return jnp.where(sudden_jumps, large_amplitude_trace, faint_amplitude_trace).astype(jnp.float32)


def shard_levels(stream_key, shape, shards, low, top_value):
    factor_of = 1.0
    for dim, blocks in shards:
        steps = jax.random.uniform(jax.random.fold_in(jax.random.fold_in(stream_key, 6), dim), (blocks,), jnp.float32, low / len(shards), top_value / len(shards))
        factor_of = factor_of * jnp.repeat(jnp.exp(steps), shape[dim] // blocks).reshape((-1,) + (1,) * (len(shape) - 1 - dim))
    return factor_of


def noise(own_key, dims, width, bound, cuts=(), kind=jnp.bfloat16):
    values = jax.random.normal(own_key, dims, jnp.float32) * width
    if len(cuts) > 0:
        values = shard_levels(own_key, dims, cuts, -0.22, 0.18) * values
    return jnp.clip(values, min=-bound, max=bound).astype(kind)


def setup_inputs(seed: int = 0) -> dict:
    keys = jax.random.split(jax.random.key(seed), 16)
    latent = noise(keys[0], (GRID_ROW_COUNT, GRID_COLUMN_COUNT, D), 1.0, 6.0, ((0, 8), (1, 16)))
    well_logs = noise(keys[1], (NCOND, D), 1.0, 6.0, ((0, 128),))
    cond_weight = noise(keys[2], (D, D), D ** -0.5, 0.375)
    trace_rows = draw_trace_rows(jax.random.fold_in(keys[15], 71), 0)
    norm_gain = jnp.clip(1.0 + 0.1 * jax.random.normal(keys[4], (D,), jnp.float32), 0.5, 1.5)
    in_weight = noise(keys[5], (D, 2 * E), D ** -0.5, 0.375)
    conv_weight = noise(keys[6], (9, E), 9 ** -0.5, 2.0, (), jnp.float32)
    bc_weight = noise(keys[7], (E, 8 * STATE), E ** -0.5, 0.375)
    dt_weight = noise(keys[8], (E, 4 * HEADS), E ** -0.5, 0.375)
    dt_bias = jnp.clip(jax.random.uniform(keys[9], (4, HEADS), jnp.float32, -0.5, 0.5), -0.5, 0.5)
    row_rate = draw_row_rate(jax.random.fold_in(keys[15], 71), 0)
    col_rate = draw_col_rate(jax.random.fold_in(keys[15], 71), 0)
    horizon = draw_horizon(jax.random.fold_in(keys[15], 71), 0)
    out_gain = jnp.clip(1.0 + 0.1 * jax.random.normal(keys[13], (E,), jnp.float32), 0.5, 1.5)
    out_weight = noise(keys[14], (E, D), E ** -0.5, 0.375)
    return dict(latent=latent, well_logs=well_logs, cond_weight=cond_weight, trace_rows=trace_rows, norm_gain=norm_gain, in_weight=in_weight, conv_weight=conv_weight, bc_weight=bc_weight, dt_weight=dt_weight, dt_bias=dt_bias, row_rate=row_rate, col_rate=col_rate, horizon=horizon, out_gain=out_gain, out_weight=out_weight)


precise = lax.Precision.HIGHEST

def segment_recurrence(states, pieces):
    signal, in_coef, out_coef, step_size, log_decay = pieces
    block_len = signal.shape[1]
    cumulative = jnp.cumsum(log_decay, axis=1)
    scores = jnp.einsum('lks,ljs->lkj', out_coef, in_coef, preferred_element_type=jnp.float32)
    driven = signal.astype(jnp.float32) * step_size[..., None]
    causal = jnp.arange(block_len)[:, None] >= jnp.arange(block_len)[None, :]

    def head_term(head_args):
        head_cum, head_drive = head_args
        spread = jnp.where(causal, head_cum[:, :, None] - head_cum[:, None, :], -jnp.inf)
        return jnp.einsum('lkj,ljp->lkp', scores * jnp.exp(spread), head_drive, precision=precise)
    inner = lax.map(head_term, (jnp.moveaxis(cumulative, 2, 0), jnp.moveaxis(driven, 2, 0)))
    inner = jnp.moveaxis(inner, 0, 2)
    carried_in = jnp.exp(cumulative)[..., None] * jnp.einsum('lks,lhps->lkhp', out_coef.astype(jnp.float32), states, precision=precise)
    tail_decay = jnp.exp(cumulative[:, -1:, :] - cumulative)
    states = jnp.exp(cumulative[:, -1, :])[:, :, None, None] * states + jnp.einsum('lkhp,lks->lhps', driven * tail_decay[..., None], in_coef.astype(jnp.float32), precision=precise)
    output = inner + carried_in
    return (states, output.reshape(output.shape[0], block_len, -1))

def line_scan(signal, in_coef, out_coef, step_size, log_decay, states):
    line_count = signal.shape[0]
    length = signal.shape[1]
    block_len = min(64, length)
    blocks = length // block_len

    def split_blocks(array):
        shaped = array.reshape((line_count, blocks, block_len) + array.shape[2:])
        return jnp.moveaxis(shaped, 1, 0)
    pieces = (split_blocks(signal), split_blocks(in_coef), split_blocks(out_coef), split_blocks(step_size), split_blocks(log_decay))
    states, outputs = lax.scan(segment_recurrence, states, pieces)
    outputs = jnp.moveaxis(outputs, 0, 1).reshape(line_count, length, -1)
    return (outputs, states)

def orient(array, along_columns, backward):
    if along_columns:
        array = jnp.swapaxes(array, 0, 1)
    if backward:
        array = jnp.flip(array, 1)
    return array

def restore(array, along_columns, backward):
    if backward:
        array = jnp.flip(array, 1)
    if along_columns:
        array = jnp.swapaxes(array, 0, 1)
    return array

def reference(latent, well_logs, cond_weight, trace_rows, norm_gain, in_weight, conv_weight, bc_weight, dt_weight, dt_bias, row_rate, col_rate, horizon, out_gain, out_weight):
    tokens = jax.nn.silu(jnp.dot(well_logs, cond_weight, preferred_element_type=jnp.float32)).astype(jnp.bfloat16)
    column_tokens = jnp.take(tokens, trace_rows, axis=0).astype(jnp.float32)
    hidden = latent.astype(jnp.float32) + column_tokens[None, :, :]
    normed = (hidden * lax.rsqrt(lax.optimization_barrier(jnp.mean(hidden * hidden, axis=-1, keepdims=True)) + 1e-06) * norm_gain).astype(jnp.bfloat16)
    projected = jnp.dot(normed.reshape(-1, D), in_weight, preferred_element_type=jnp.float32).astype(jnp.bfloat16).reshape(GRID_ROW_COUNT, GRID_COLUMN_COUNT, 2 * E)
    pre_conv = projected[..., :E]
    gating_share = projected[..., E:]
    padded = jnp.pad(pre_conv, ((1, 1), (1, 1), (0, 0)))
    conv_sum = jnp.zeros((GRID_ROW_COUNT, GRID_COLUMN_COUNT, E), jnp.float32)
    for offset_row in range(3):
        for offset_col in range(3):
            conv_sum = conv_sum + padded[offset_row:offset_row + GRID_ROW_COUNT, offset_col:offset_col + GRID_COLUMN_COUNT].astype(jnp.float32) * conv_weight[3 * offset_row + offset_col]
    mixed_x = jax.nn.silu(conv_sum).astype(jnp.bfloat16)
    flat_x = mixed_x.reshape(-1, E)
    step_size = jax.nn.softplus(jnp.dot(flat_x, dt_weight, preferred_element_type=jnp.float32).reshape(GRID_ROW_COUNT, GRID_COLUMN_COUNT, 4, HEADS) + dt_bias)
    rates_all = jnp.concatenate([row_rate / (16.0 * GRID_COLUMN_COUNT), col_rate / (16.0 * GRID_ROW_COUNT)], 0)
    log_decay = -step_size * rates_all - horizon[:, :, None, None]
    signal = mixed_x.reshape(GRID_ROW_COUNT, GRID_COLUMN_COUNT, HEADS, HEAD_DIM)
    total = jnp.zeros((GRID_ROW_COUNT, GRID_COLUMN_COUNT, E), jnp.float32)
    for direction in range(4):
        coef_pair = jnp.dot(flat_x, bc_weight[:, direction * 2 * STATE:(direction + 1) * 2 * STATE], preferred_element_type=jnp.float32).astype(jnp.bfloat16).reshape(GRID_ROW_COUNT, GRID_COLUMN_COUNT, 2 * STATE)
        along_columns = direction >= 2
        backward = direction % 2 == 1
        signal_l = orient(signal, along_columns, backward)
        in_l = orient(coef_pair[..., :STATE], along_columns, backward)
        out_l = orient(coef_pair[..., STATE:], along_columns, backward)
        step_l = orient(step_size[:, :, direction], along_columns, backward)
        decay_l = orient(log_decay[:, :, direction], along_columns, backward)
        zero_states = jnp.zeros((signal_l.shape[0], HEADS, HEAD_DIM, STATE), jnp.float32)
        outputs = line_scan(signal_l, in_l, out_l, step_l, decay_l, zero_states)[0]
        total = total + restore(outputs, along_columns, backward)
    gated = (total * lax.rsqrt(lax.optimization_barrier(jnp.mean(total * total, axis=-1, keepdims=True)) + 1e-05) * out_gain * jax.nn.silu(gating_share.astype(jnp.float32))).astype(jnp.bfloat16)
    branch = jnp.dot(gated.reshape(-1, E), out_weight, preferred_element_type=jnp.float32).reshape(GRID_ROW_COUNT, GRID_COLUMN_COUNT, D)
    return (hidden + branch).astype(jnp.bfloat16)
```

```python
import jax
import jax.numpy as jnp
from jax import lax
from jax.experimental import pallas as pl
from jax.experimental.pallas import tpu as pltpu
from jax.sharding import PartitionSpec as P

F32 = jnp.float32
BF16 = jnp.bfloat16
ROWS = 8
COLS = 16
TR = 16
TC = 8
LINE = 128
D = 256
HEADS = 16
HEAD_DIM = 16
STATE = 128
precise = lax.Precision.HIGHEST


def iota(shape, dim):
    return lax.broadcasted_iota(jnp.int32, shape, dim)


def halves(x):
    high = x.astype(BF16).astype(F32)
    return high, x - high


def silu(x):
    return x * jax.nn.sigmoid(x)


def pack_row_kernel(latent_ref, logs_ref, horizon_ref, out_ref):
    r = lax.axis_index("row")
    target = iota((LINE, LINE), 0)
    source = iota((LINE, LINE), 1)
    pick = ((target % TR) * TC + target // TR == source).astype(BF16)
    flat = latent_ref[...].astype(F32).reshape(LINE, D).astype(BF16)
    columns = jnp.dot(pick, flat, preferred_element_type=F32).astype(BF16)
    halo = jnp.concatenate(
        [latent_ref[0].astype(F32), latent_ref[TR - 1].astype(F32)], axis=0
    ).astype(BF16)
    row8 = iota((8, D), 0)
    logs = jnp.where(row8 == r, jnp.broadcast_to(logs_ref[...].astype(F32), (8, D)), 0.0)
    here = iota((TR, LINE), 1) - TR * r == iota((TR, LINE), 0)
    for dest in range(ROWS):
        for slot in range(3):
            j = (dest + slot - 1) % ROWS
            out_ref[dest, slot * TR : (slot + 1) * TR, :] = columns[j * TR : (j + 1) * TR, :]
        out_ref[dest, 48:64, :] = halo
        column = jnp.broadcast_to(horizon_ref[:, dest : dest + 1], (TR, LINE))
        line = jnp.sum(jnp.where(here, column, 0.0), axis=0, keepdims=True)
        high, low = halves(line)
        meta = jnp.concatenate([high, low], axis=1)
        meta = jnp.where(row8 == 0, jnp.broadcast_to(meta, (8, D)), 0.0)
        out_ref[dest, 64:80, :] = jnp.concatenate([logs, meta], axis=0).astype(BF16)


def pack_col_kernel(trace_ref, got_ref, latent_ref, horizon_ref, out_ref, side_ref):
    r = lax.axis_index("row")
    c = lax.axis_index("col")
    above = got_ref[jnp.maximum(r - 1, 0), 48:64, :].astype(F32)[8:16]
    below = got_ref[jnp.minimum(r + 1, ROWS - 1), 48:64, :].astype(F32)[0:8]
    own = latent_ref[...].astype(F32)
    logs = jnp.sum(got_ref[:, 64:80, :].astype(F32)[:, 0:8, :], axis=0)
    lane = iota((TR, LINE), 1) - TC * c
    spread = jnp.zeros((TR, LINE), F32)
    lane1 = iota((1, LINE), 1) - TC * c
    trace = jnp.zeros((1, LINE), F32)
    for j in range(TC):
        column = jnp.broadcast_to(horizon_ref[:, j : j + 1], (TR, LINE))
        spread = jnp.where(lane == j, column, spread)
        trace = jnp.where(lane1 == j, trace_ref[j].astype(F32), trace)
    high, low = halves(spread)
    first = jnp.concatenate([jnp.broadcast_to(trace, (TR, LINE)), high], axis=1)
    second = jnp.concatenate([low, jnp.zeros((TR, LINE), F32)], axis=1)
    row16 = iota((16, D), 0)
    rows = [above] + [own[i] for i in range(TR)] + [below]
    for dest in range(COLS):
        pair = jnp.concatenate([rows[dest], rows[dest + 1]], axis=0)
        out_ref[dest, 0:16, :] = pair.astype(BF16)
        pair = jnp.concatenate([rows[dest + 2], logs], axis=0)
        out_ref[dest, 16:32, :] = pair.astype(BF16)
        meta = jnp.where(row16 == 0, jnp.broadcast_to(first[dest : dest + 1], (16, D)), 0.0)
        meta = jnp.where(row16 == 1, jnp.broadcast_to(second[dest : dest + 1], (16, D)), meta)
        out_ref[dest, 32:48, :] = meta.astype(BF16)
    left = got_ref[:, 0:16, :]
    right = got_ref[:, 32:48, :]
    side_ref[...] = jnp.where(r == 0, left, right)


def normalised(hidden, gain):
    scale = lax.rsqrt(jnp.mean(hidden * hidden, axis=-1, keepdims=True) + 1e-06)
    return (hidden * scale * gain).astype(BF16)


def line_scan(cells, tokens, inside, taps, gain, in_w, bc, dt_w, bias, rate, horizon, w_ref, x_ref):
    pre = []
    for s in range(3):
        n = normalised(cells[s] + tokens[s], gain)
        p = jnp.dot(n, in_w, preferred_element_type=F32).astype(BF16).astype(F32)
        pre.append(jnp.where(inside[s], p, 0.0))
    shifted = [
        taps[t][0] * pre[0] + taps[t][1] * pre[1] + taps[t][2] * pre[2] for t in range(3)
    ]
    place = iota((LINE, D), 0)
    conv = (
        shifted[1]
        + jnp.where(place == 0, 0.0, pltpu.roll(shifted[0], 1, 0))
        + jnp.where(place == LINE - 1, 0.0, pltpu.roll(shifted[2], LINE - 1, 0))
    )
    mixed = silu(conv).astype(BF16)
    coef = jnp.dot(mixed, bc, preferred_element_type=F32).astype(BF16)
    contract = (((1,), (1,)), ((), ()))
    k = iota((LINE, LINE), 0)
    j = iota((LINE, LINE), 1)
    lower = j <= k
    score_f = lax.dot_general(
        coef[:, STATE : 2 * STATE], coef[:, :STATE], contract, preferred_element_type=F32
    )
    score_b = lax.dot_general(
        coef[:, 3 * STATE :], coef[:, 2 * STATE : 3 * STATE], contract, preferred_element_type=F32
    )
    score_f = jnp.where(lower, score_f, 0.0)
    score_b = jnp.where(j >= k, score_b, 0.0)
    steps = []
    sums_t = []
    sums = []
    for side in range(2):
        z = jnp.dot(mixed, dt_w[side], preferred_element_type=F32) + bias[side]
        step = jnp.maximum(z, 0.0) + jnp.log1p(jnp.exp(-jnp.abs(z)))
        decay_t = (-step * rate[side]).T - horizon
        ones = (k <= j) if side == 0 else (k >= j)
        total = jnp.dot(decay_t, ones.astype(F32), precision=precise, preferred_element_type=F32)
        steps.append(step.T)
        sums_t.append(total)
        sums.append(total.T)
    head_of = iota((LINE, D), 1) // HEAD_DIM
    wide = mixed.astype(F32)
    for h in range(HEADS):
        ahead = sums[0][:, h : h + 1] - sums_t[0][h : h + 1, :]
        behind = sums[1][:, h : h + 1] - sums_t[1][h : h + 1, :]
        decay = jnp.exp(jnp.where(lower, ahead, behind))
        drive = score_f * steps[0][h : h + 1, :] + score_b * steps[1][h : h + 1, :]
        w_ref[:, h * LINE : (h + 1) * LINE] = (drive * decay).astype(BF16)
        x_ref[h * LINE : (h + 1) * LINE, :] = jnp.where(head_of == h, wide, 0.0).astype(BF16)
    return jnp.dot(w_ref[...], x_ref[...], preferred_element_type=F32)


def column_kernel(
    rows_ref,
    side_ref,
    cols_ref,
    cond_ref,
    gain_ref,
    in_ref,
    conv_ref,
    bc_ref,
    dt_ref,
    bias_ref,
    rate_ref,
    out_ref,
    tokens_ref,
    w_ref,
    x_ref,
):
    r = lax.axis_index("row")
    c = lax.axis_index("col")
    logs = cols_ref[:, 16:32, :].astype(F32)[:, 8:16, :].reshape(LINE, D).astype(BF16)
    tokens = silu(jnp.dot(logs, cond_ref[...], preferred_element_type=F32)).astype(BF16)
    meta = jnp.sum(cols_ref[:, 32:48, :].astype(F32), axis=0)
    trace = meta[0:1, 0:LINE].astype(jnp.int32)
    position = iota((LINE, LINE), 0)
    names = (position % ROWS) * COLS + position // ROWS
    chosen = (names == trace).astype(F32).T.astype(BF16)
    tokens_ref[...] = jnp.dot(chosen, tokens, preferred_element_type=F32)
    column = c * TC + r
    cells = [
        rows_ref[:, s * TR : (s + 1) * TR, :].astype(F32).reshape(LINE, D) for s in range(3)
    ]
    side = side_ref[...].astype(F32).reshape(LINE, D)
    cells[0] = jnp.where(r == 0, side, cells[0])
    cells[2] = jnp.where(r == ROWS - 1, side, cells[2])
    lines = [jnp.maximum(column - 1, 0), column, jnp.minimum(column + 1, LINE - 1)]
    line_tokens = [tokens_ref[pl.ds(x, 1), :] for x in lines]
    hor = jnp.sum(rows_ref[:, 64:80, :].astype(F32), axis=0)[8:9]
    horizon = hor[:, :LINE] + hor[:, LINE:]
    out_ref[...] = line_scan(
        cells,
        line_tokens,
        [column > 0, True, column < LINE - 1],
        [[conv_ref[3 * t + s : 3 * t + s + 1, :] for s in range(3)] for t in range(3)],
        gain_ref[...],
        in_ref[:, :D],
        bc_ref[:, 4 * STATE :],
        [dt_ref[:, 2 * HEADS : 3 * HEADS], dt_ref[:, 3 * HEADS :]],
        [bias_ref[2:3, :], bias_ref[3:4, :]],
        [rate_ref[0:1, :] / 2048.0, rate_ref[1:2, :] / 2048.0],
        horizon,
        w_ref,
        x_ref,
    ).astype(BF16)


def row_kernel(
    cols_ref,
    tokens_ref,
    gain_ref,
    in_ref,
    conv_ref,
    bc_ref,
    dt_ref,
    bias_ref,
    rate_ref,
    out_ref,
    w_ref,
    x_ref,
):
    r = lax.axis_index("row")
    c = lax.axis_index("col")
    row = r * TR + c
    pair = cols_ref[:, 0:16, :].astype(F32)
    last = cols_ref[:, 16:32, :].astype(F32)
    cells = [pair[:, 0:8, :], pair[:, 8:16, :], last[:, 0:8, :]]
    cells = [x.reshape(LINE, D) for x in cells]
    tokens = tokens_ref[...]
    meta = jnp.sum(cols_ref[:, 32:48, :].astype(F32), axis=0)
    horizon = meta[0:1, LINE:] + meta[1:2, :LINE]
    out_ref[...] = line_scan(
        cells,
        [tokens, tokens, tokens],
        [row > 0, True, row < LINE - 1],
        [[conv_ref[3 * s + t : 3 * s + t + 1, :] for s in range(3)] for t in range(3)],
        gain_ref[...],
        in_ref[:, :D],
        bc_ref[:, : 4 * STATE],
        [dt_ref[:, :HEADS], dt_ref[:, HEADS : 2 * HEADS]],
        [bias_ref[0:1, :], bias_ref[1:2, :]],
        [rate_ref[0:1, :] / 2048.0, rate_ref[1:2, :] / 2048.0],
        horizon,
        w_ref,
        x_ref,
    ).astype(BF16)


def tile_kernel(latent_ref, tokens_ref, gain_ref, in_ref, hidden_ref, gate_ref):
    c = lax.axis_index("col")
    own = tokens_ref[pl.ds(c * TC, TC), :]
    hidden = (latent_ref[...].astype(F32) + own[None]).reshape(LINE, D)
    hidden_ref[...] = hidden
    n = normalised(hidden, gain_ref[...])
    gate = jnp.dot(n, in_ref[:, D:], preferred_element_type=F32).astype(BF16).astype(F32)
    gate_ref[...] = silu(gate)


def finish_kernel(row_ref, col_ref, hidden_ref, gate_ref, gain_ref, out_w_ref, out_ref):
    target = iota((LINE, LINE), 0)
    source = iota((LINE, LINE), 1)
    pick = ((target % TC) * TR + target // TC == source).astype(BF16)
    by_column = jnp.dot(pick, col_ref[...].reshape(LINE, D), preferred_element_type=F32)
    total = row_ref[...].astype(F32).reshape(LINE, D) + by_column
    scale = lax.rsqrt(jnp.mean(total * total, axis=-1, keepdims=True) + 1e-05)
    gated = (total * scale * gain_ref[...] * gate_ref[...]).astype(BF16)
    branch = jnp.dot(gated, out_w_ref[...], preferred_element_type=F32)
    out_ref[...] = (hidden_ref[...] + branch).reshape(TR, TC, D).astype(BF16)


def call(kernel, outs, *args, scratch=(), smem_first=False):
    vmem = pl.BlockSpec(memory_space=pltpu.VMEM)
    specs = [vmem] * len(args)
    if smem_first:
        specs[0] = pl.BlockSpec(memory_space=pltpu.SMEM)
    return pl.pallas_call(
        kernel,
        out_shape=[jax.ShapeDtypeStruct(s, d) for s, d in outs],
        in_specs=specs,
        out_specs=[vmem] * len(outs),
        scratch_shapes=list(scratch),
        name=kernel.__name__,
    )(*args)


def per_device(
    latent,
    well_logs,
    cond_weight,
    trace_rows,
    norm_gain,
    in_weight,
    conv_weight,
    bc_weight,
    dt_weight,
    dt_bias,
    row_rate,
    col_rate,
    horizon,
    out_gain,
    out_weight,
):
    gain = norm_gain.reshape(1, D)
    final_gain = out_gain.reshape(1, D)
    (packed,) = call(
        pack_row_kernel, [((ROWS, 80, D), BF16)], latent, well_logs, horizon
    )
    from_rows = lax.all_to_all(packed, "row", 0, 0, tiled=True)
    packed, side = call(
        pack_col_kernel,
        [((COLS, 48, D), BF16), ((ROWS, TR, D), BF16)],
        trace_rows,
        from_rows,
        latent,
        horizon,
        smem_first=True,
    )
    neighbours = [(i, i + 1) for i in range(COLS - 1)]
    last = (ROWS - 1) * COLS
    neighbours += [(last + i + 1, last + i) for i in range(COLS - 1)]
    side = lax.ppermute(side, ("row", "col"), neighbours)
    from_cols = lax.all_to_all(packed, "col", 0, 0, tiled=True)
    scratch = [pltpu.VMEM((LINE, HEADS * LINE), BF16), pltpu.VMEM((HEADS * LINE, D), BF16)]
    by_column, tokens = call(
        column_kernel,
        [((LINE, D), BF16), ((LINE, D), F32)],
        from_rows,
        side,
        from_cols,
        cond_weight,
        gain,
        in_weight,
        conv_weight,
        bc_weight,
        dt_weight,
        dt_bias,
        col_rate,
        scratch=scratch,
    )
    by_column = lax.all_to_all(by_column.reshape(ROWS, TR, D), "row", 0, 0, tiled=True)
    (by_row,) = call(
        row_kernel,
        [((LINE, D), BF16)],
        from_cols,
        tokens,
        gain,
        in_weight,
        conv_weight,
        bc_weight,
        dt_weight,
        dt_bias,
        row_rate,
        scratch=scratch,
    )
    by_row = lax.all_to_all(by_row.reshape(COLS, TC, D), "col", 0, 0, tiled=True)
    hidden, gate = call(
        tile_kernel, [((LINE, D), F32), ((LINE, D), F32)], latent, tokens, gain, in_weight
    )
    (out,) = call(
        finish_kernel,
        [((TR, TC, D), BF16)],
        by_row,
        by_column,
        hidden,
        gate,
        final_gain,
        out_weight,
    )
    return out


def solution(mesh):
    placed = (
        P("row", "col", None),
        P(("row", "col"), None),
        P(),
        P("col"),
        P(),
        P(),
        P(),
        P(),
        P(),
        P(),
        P(),
        P(),
        P("row", "col"),
        P(),
        P(),
    )
    return jax.shard_map(
        per_device, mesh=mesh, in_specs=placed, out_specs=P("row", "col", None), check_vma=False
    )
```

```python
import jax
import jax.numpy as jnp
from jax import lax
from jax.experimental import pallas as pl
from jax.experimental.pallas import tpu as pltpu
from jax.sharding import PartitionSpec as P

F32 = jnp.float32
BF16 = jnp.bfloat16
ROWS = 8
COLS = 16
TR = 16
TC = 8
LINE = 128
D = 256
HEADS = 16
HEAD_DIM = 16
STATE = 128


def iota(shape, dim):
    return lax.broadcasted_iota(jnp.int32, shape, dim)


def halves(x):
    high = x.astype(BF16).astype(F32)
    return high, x - high


def silu(x):
    return x * jax.nn.sigmoid(x)


def pack_row_kernel(trace_ref, latent_ref, logs_ref, horizon_ref, out_ref, meta_ref, own_ref):
    r = lax.axis_index("row")
    c = lax.axis_index("col")
    own_ref[...] = latent_ref[...]
    target = iota((LINE, LINE), 0)
    source = iota((LINE, LINE), 1)
    pick = ((target % TR) * TC + target // TR == source).astype(BF16)
    flat = latent_ref[...].astype(F32).reshape(LINE, D).astype(BF16)
    columns = jnp.dot(pick, flat, preferred_element_type=F32).astype(BF16)
    halo = jnp.concatenate(
        [latent_ref[0].astype(F32), latent_ref[TR - 1].astype(F32)], axis=0
    ).astype(BF16)
    logs = jnp.where(iota((8, D), 0) == r, jnp.broadcast_to(logs_ref[...].astype(F32), (8, D)), 0.0)
    high, low = halves(horizon_ref[...])
    here = (iota((TR, LINE), 1) - TR * r == iota((TR, LINE), 0)).astype(BF16)
    lines = jnp.concatenate(
        [
            jnp.dot(high.astype(BF16), here, preferred_element_type=F32),
            jnp.dot(low.astype(BF16), here, preferred_element_type=F32),
        ],
        axis=1,
    )
    meta = jnp.concatenate([logs, lines], axis=0).astype(BF16)
    for dest in range(ROWS):
        out_ref[dest, 0:128, :] = columns
        out_ref[dest, 128:144, :] = halo
        out_ref[dest, 144:160, :] = meta
    lane = iota((TR, LINE), 1) - TC * c
    lane1 = iota((1, LINE), 1) - TC * c
    spread = jnp.zeros((TR, LINE), F32)
    trace = jnp.zeros((1, LINE), F32)
    across = horizon_ref[...].T
    for j in range(TC):
        column = jnp.broadcast_to(across[:, j : j + 1], (TR, LINE))
        spread = jnp.where(lane == j, column, spread)
        trace = jnp.where(lane1 == j, trace_ref[j].astype(F32), trace)
    high, low = halves(spread)
    first = jnp.concatenate([jnp.broadcast_to(trace, (TR, LINE)), high], axis=1)
    second = jnp.concatenate([low, jnp.zeros((TR, LINE), F32)], axis=1)
    row8 = iota((8, D), 0)
    for dest in range(COLS):
        part = jnp.where(row8 == 0, jnp.broadcast_to(first[dest : dest + 1], (8, D)), 0.0)
        part = jnp.where(row8 == 1, jnp.broadcast_to(second[dest : dest + 1], (8, D)), part)
        meta_ref[dest] = part.astype(BF16)


def pack_col_kernel(got_ref, own_ref, meta_ref, out_ref, left_ref, right_ref):
    r = lax.axis_index("row")
    above = got_ref[jnp.maximum(r - 1, 0), 128:144, :].astype(F32)[8:16]
    below = got_ref[jnp.minimum(r + 1, ROWS - 1), 128:144, :].astype(F32)[0:8]
    own = own_ref[...].astype(F32)
    logs = jnp.sum(got_ref[:, 144:160, :].astype(F32)[:, 0:8, :], axis=0)
    rows = [above] + [own[i] for i in range(TR)] + [below]
    for dest in range(COLS):
        pair = jnp.concatenate([rows[dest], rows[dest + 1]], axis=0)
        out_ref[dest, 0:16, :] = pair.astype(BF16)
        pair = jnp.concatenate([rows[dest + 2], logs], axis=0)
        out_ref[dest, 16:32, :] = pair.astype(BF16)
        out_ref[dest, 32:40, :] = meta_ref[dest]
    left_ref[...] = got_ref[:, 0:16, :]
    right_ref[...] = got_ref[:, 112:128, :]


def params_kernel(gate_ref, gain_ref, last_ref, conv_ref, bias_ref, row_ref, col_ref, wide_ref, side_ref):
    wide_ref[0:9, :] = conv_ref[...]
    wide_ref[9:10, :] = gain_ref[...]
    wide_ref[10:11, :] = last_ref[...]
    bias = bias_ref[...].T
    rates = [row_ref[...].T / 2048.0, col_ref[...].T / 2048.0]
    for k in range(4):
        side_ref[0, k * HEADS : (k + 1) * HEADS, :] = jnp.broadcast_to(
            bias[:, k : k + 1], (HEADS, LINE)
        )
        side_ref[1, k * HEADS : (k + 1) * HEADS, :] = jnp.broadcast_to(
            rates[k // 2][:, k % 2 : k % 2 + 1], (HEADS, LINE)
        )


def normalised(hidden, gain):
    scale = lax.rsqrt(jnp.mean(hidden * hidden, axis=-1, keepdims=True) + 1e-06)
    return (hidden * scale * gain).astype(BF16)


def line_scan(cells, tokens, inside, taps, gain, in_w, bc, dt_w, bias, rate, horizon, w_ref, x_ref):
    pre = []
    for s in range(3):
        n = normalised(cells[s] + tokens[s], gain)
        p = jnp.dot(n, in_w, preferred_element_type=F32).astype(BF16).astype(F32)
        pre.append(jnp.where(inside[s], p, 0.0))
    shifted = [
        taps[t][0] * pre[0] + taps[t][1] * pre[1] + taps[t][2] * pre[2] for t in range(3)
    ]
    place = iota((LINE, D), 0)
    conv = (
        shifted[1]
        + jnp.where(place == 0, 0.0, pltpu.roll(shifted[0], 1, 0))
        + jnp.where(place == LINE - 1, 0.0, pltpu.roll(shifted[2], LINE - 1, 0))
    )
    mixed = silu(conv).astype(BF16)
    coef = jnp.dot(mixed, bc, preferred_element_type=F32).astype(BF16)
    contract = (((1,), (1,)), ((), ()))
    k = iota((LINE, LINE), 0)
    j = iota((LINE, LINE), 1)
    lower = j <= k
    score_f = lax.dot_general(
        coef[:, STATE : 2 * STATE], coef[:, :STATE], contract, preferred_element_type=F32
    )
    score_b = lax.dot_general(
        coef[:, 3 * STATE :], coef[:, 2 * STATE : 3 * STATE], contract, preferred_element_type=F32
    )
    score_f = jnp.where(lower, score_f, 0.0)
    score_b = jnp.where(j >= k, score_b, 0.0)
    steps = []
    sums_t = []
    sums = []
    for side in range(2):
        z = lax.dot_general(dt_w[side], mixed, contract, preferred_element_type=F32) + bias[side]
        step = jnp.maximum(z, 0.0) + jnp.log1p(jnp.exp(-jnp.abs(z)))
        decay = -step * rate[side] - horizon
        ones = ((k <= j) if side == 0 else (k >= j)).astype(BF16)
        high, rest = halves(decay)
        middle, low = halves(rest)
        parts = jnp.concatenate([high, middle, low], axis=0).astype(BF16)
        total = jnp.dot(parts, ones, preferred_element_type=F32)
        total = total[:HEADS] + (total[HEADS : 2 * HEADS] + total[2 * HEADS :])
        steps.append(step)
        sums_t.append(total)
        sums.append(total.T)
    head_of = iota((LINE, D), 1) // HEAD_DIM
    wide = mixed.astype(F32)
    for h in range(HEADS):
        ahead = sums[0][:, h : h + 1] - sums_t[0][h : h + 1, :]
        behind = sums[1][:, h : h + 1] - sums_t[1][h : h + 1, :]
        decay = jnp.exp(jnp.where(lower, ahead, behind))
        drive = score_f * steps[0][h : h + 1, :] + score_b * steps[1][h : h + 1, :]
        w_ref[:, h * LINE : (h + 1) * LINE] = (drive * decay).astype(BF16)
        x_ref[h * LINE : (h + 1) * LINE, :] = jnp.where(head_of == h, wide, 0.0).astype(BF16)
    return jnp.dot(w_ref[...], x_ref[...], preferred_element_type=F32)


def row_kernel(
    cols_ref,
    wide_ref,
    side_ref,
    cond_ref,
    in_ref,
    bc_ref,
    dt_ref,
    out_ref,
    tokens_ref,
    w_ref,
    x_ref,
):
    r = lax.axis_index("row")
    c = lax.axis_index("col")
    pair = cols_ref[:, 0:16, :].astype(F32)
    last = cols_ref[:, 16:32, :].astype(F32)
    logs = last[:, 8:16, :].reshape(LINE, D).astype(BF16)
    tokens = silu(jnp.dot(logs, cond_ref[...], preferred_element_type=F32)).astype(BF16)
    meta = jnp.sum(cols_ref[:, 32:40, :].astype(F32), axis=0)
    trace = meta[0:1, 0:LINE].astype(jnp.int32)
    position = iota((LINE, LINE), 0)
    names = (position % ROWS) * COLS + position // ROWS
    chosen = (names == trace).astype(F32).T.astype(BF16)
    tokens = jnp.dot(chosen, tokens, preferred_element_type=F32)
    tokens_ref[...] = tokens
    row = r * TR + c
    cells = [pair[:, 0:8, :], pair[:, 8:16, :], last[:, 0:8, :]]
    cells = [x.reshape(LINE, D) for x in cells]
    out_ref[...] = line_scan(
        cells,
        [tokens, tokens, tokens],
        [row > 0, True, row < LINE - 1],
        [[wide_ref[3 * s + t : 3 * s + t + 1, :] for s in range(3)] for t in range(3)],
        wide_ref[9:10, :],
        in_ref[:, :D],
        bc_ref[:, : 4 * STATE],
        [dt_ref[:HEADS, :], dt_ref[HEADS : 2 * HEADS, :]],
        [side_ref[0, :HEADS, :], side_ref[0, HEADS : 2 * HEADS, :]],
        [side_ref[1, :HEADS, :], side_ref[1, HEADS : 2 * HEADS, :]],
        meta[0:1, LINE:] + meta[1:2, :LINE],
        w_ref,
        x_ref,
    ).astype(BF16)


def column_kernel(
    rows_ref,
    left_ref,
    right_ref,
    tokens_ref,
    own_ref,
    wide_ref,
    side_ref,
    in_ref,
    bc_ref,
    dt_ref,
    hidden_ref,
    gate_ref,
    sum_ref,
    normed_ref,
    pre_ref,
    mixed_ref,
    b_ref,
    cum_ref,
    w_ref,
    y_ref,
):
    r = lax.axis_index("row")
    c = lax.axis_index("col")
    gain = wide_ref[9:10, :]
    hidden = own_ref[...].astype(F32) + tokens_ref[pl.ds(pl.multiple_of(c * TC, TC), TC), :][None]
    hidden = hidden.reshape(LINE, D)
    hidden_ref[...] = hidden
    gate = jnp.dot(normalised(hidden, gain), in_ref[:, D:], preferred_element_type=F32)
    gate_ref[...] = silu(gate.astype(BF16).astype(F32))
    for q in range(TC + 2):
        if q == 0:
            cells = left_ref[...]
        elif q == TC + 1:
            cells = right_ref[...]
        else:
            cells = rows_ref[:, (q - 1) * TR : q * TR, :]
        line = jnp.clip(c * TC + q - 1, 0, LINE - 1)
        cells = cells.astype(F32).reshape(LINE, D) + tokens_ref[pl.ds(line, 1), :]
        normed_ref[q * LINE : (q + 1) * LINE, :] = normalised(cells, gain)
    pre_ref[...] = jnp.dot(
        normed_ref[...], in_ref[:, :D], preferred_element_type=F32
    ).astype(BF16)
    place = iota((LINE, D), 0)
    inside = [c > 0] + [True] * TC + [c < COLS - 1]
    for j in range(TC):
        pre = []
        for s in range(3):
            p = pre_ref[(j + s) * LINE : (j + s + 1) * LINE, :].astype(F32)
            pre.append(p if inside[j + s] is True else jnp.where(inside[j + s], p, 0.0))
        shifted = [
            sum(wide_ref[3 * a + s : 3 * a + s + 1, :] * pre[s] for s in range(3))
            for a in range(3)
        ]
        conv = (
            shifted[1]
            + jnp.where(place == 0, 0.0, pltpu.roll(shifted[0], 1, 0))
            + jnp.where(place == LINE - 1, 0.0, pltpu.roll(shifted[2], LINE - 1, 0))
        )
        mixed_ref[j * LINE : (j + 1) * LINE, :] = silu(conv).astype(BF16)
    base = 4 * STATE
    b_weight = jnp.concatenate(
        [bc_ref[:, base : base + STATE], bc_ref[:, base + 2 * STATE : base + 3 * STATE]], axis=1
    )
    c_weight = jnp.concatenate(
        [bc_ref[:, base + STATE : base + 2 * STATE], bc_ref[:, base + 3 * STATE :]], axis=1
    )
    b_ref[...] = jnp.dot(mixed_ref[...], b_weight, preferred_element_type=F32).astype(BF16)
    start = pl.multiple_of(r * TR, TR)
    mine = jnp.concatenate(
        [mixed_ref[pl.ds(j * LINE + start, TR), :] for j in range(TC)], axis=0
    )
    c_own = jnp.dot(mine, c_weight, preferred_element_type=F32).astype(BF16)
    contract = (((1,), (1,)), ((), ()))
    z = lax.dot_general(
        dt_ref[2 * HEADS :, :], mixed_ref[...], contract, preferred_element_type=F32
    )
    k = iota((LINE, LINE), 0)
    j_ = iota((LINE, LINE), 1)
    horizon = jnp.sum(rows_ref[:, 144:160, :].astype(F32), axis=0)[8:16]
    horizon = horizon[:, :LINE] + horizon[:, LINE:]
    steps = []
    sums = []
    for side in range(2):
        bias = side_ref[0, (2 + side) * HEADS : (3 + side) * HEADS, :]
        rate = side_ref[1, (2 + side) * HEADS : (3 + side) * HEADS, :]
        own_steps = []
        decays = []
        for j in range(TC):
            zj = z[side * HEADS : (side + 1) * HEADS, j * LINE : (j + 1) * LINE] + bias
            step = jnp.maximum(zj, 0.0) + jnp.log1p(jnp.exp(-jnp.abs(zj)))
            own_steps.append(step)
            decays.append(-step * rate - horizon[j : j + 1, :])
        decay = jnp.concatenate(decays, axis=0)
        ones = ((k <= j_) if side == 0 else (k >= j_)).astype(BF16)
        high, rest = halves(decay)
        middle, low = halves(rest)
        parts = jnp.concatenate([high, middle, low], axis=0).astype(BF16)
        total = jnp.dot(parts, ones, preferred_element_type=F32)
        total = total[:LINE] + (total[LINE : 2 * LINE] + total[2 * LINE :])
        cum_ref[side] = total.T
        steps.append(own_steps)
        sums.append(total)
    ahead_own = cum_ref[0, pl.ds(start, TR), :]
    behind_own = cum_ref[1, pl.ds(start, TR), :]
    at = iota((TR, LINE), 0) + start
    other = iota((TR, LINE), 1)
    lower = other <= at
    upper = other >= at
    head_of = iota((TR, D), 1) // HEAD_DIM
    for j in range(TC):
        cj = c_own[j * TR : (j + 1) * TR, :]
        bj = b_ref[j * LINE : (j + 1) * LINE, :]
        score_f = lax.dot_general(
            cj[:, :STATE], bj[:, :STATE], contract, preferred_element_type=F32
        )
        score_b = lax.dot_general(
            cj[:, STATE:], bj[:, STATE:], contract, preferred_element_type=F32
        )
        score_f = jnp.where(lower, score_f, 0.0)
        score_b = jnp.where(upper, score_b, 0.0)
        for h in range(HEADS):
            n = j * HEADS + h
            ahead = ahead_own[:, n : n + 1] - sums[0][n : n + 1, :]
            behind = behind_own[:, n : n + 1] - sums[1][n : n + 1, :]
            decay = jnp.exp(jnp.where(lower, ahead, behind))
            drive = score_f * steps[0][j][h : h + 1, :] + score_b * steps[1][j][h : h + 1, :]
            w_ref[j, h * TR : (h + 1) * TR, :] = (drive * decay).astype(BF16)
        full = jnp.dot(
            w_ref[j], mixed_ref[j * LINE : (j + 1) * LINE, :], preferred_element_type=F32
        )
        got = full[:TR, :]
        for h in range(1, HEADS):
            got = jnp.where(head_of == h, full[h * TR : (h + 1) * TR, :], got)
        y_ref[j * TR : (j + 1) * TR, :] = got
    pick = ((k % TC) * TR + k // TC == j_).astype(BF16)
    high, low = halves(y_ref[...])
    sum_ref[...] = jnp.dot(pick, high.astype(BF16), preferred_element_type=F32) + jnp.dot(
        pick, low.astype(BF16), preferred_element_type=F32
    )


def finish_kernel(row_ref, col_ref, hidden_ref, gate_ref, wide_ref, out_w_ref, out_ref):
    total = row_ref[...].astype(F32).reshape(LINE, D) + col_ref[...]
    scale = lax.rsqrt(jnp.mean(total * total, axis=-1, keepdims=True) + 1e-05)
    gated = (total * scale * wide_ref[10:11, :] * gate_ref[...]).astype(BF16)
    branch = jnp.dot(gated, out_w_ref[...], preferred_element_type=F32)
    out_ref[...] = (hidden_ref[...] + branch).reshape(TR, TC, D).astype(BF16)


def call(kernel, outs, *args, scratch=(), smem=0, pinned=True, result=False):
    vmem = pl.BlockSpec(memory_space=pltpu.VMEM)
    specs = [pl.BlockSpec(memory_space=pltpu.SMEM)] * smem + [vmem] * (len(args) - smem)
    if pinned is True:
        pinned = range(smem, len(args))
    args = [
        pltpu.with_memory_space_constraint(x, pltpu.VMEM) if i in pinned else x
        for i, x in enumerate(args)
    ]
    shape = jax.ShapeDtypeStruct if result else pltpu.VMEM
    return pl.pallas_call(
        kernel,
        out_shape=[shape(s, d) for s, d in outs],
        in_specs=specs,
        out_specs=[vmem] * len(outs),
        scratch_shapes=list(scratch),
        name=kernel.__name__,
    )(*args)


def per_device(
    latent,
    well_logs,
    cond_weight,
    trace_rows,
    norm_gain,
    in_weight,
    conv_weight,
    bc_weight,
    dt_weight,
    dt_bias,
    row_rate,
    col_rate,
    horizon,
    out_gain,
    out_weight,
):
    dt_weight = dt_weight.T
    packed, meta, own = call(
        pack_row_kernel,
        [((ROWS, 160, D), BF16), ((COLS, 8, D), BF16), ((TR, TC, D), BF16)],
        trace_rows,
        latent,
        well_logs,
        horizon.T,
        smem=1,
        pinned=(),
    )
    from_rows = lax.all_to_all(packed, "row", 0, 0, tiled=True)
    packed, first, last = call(
        pack_col_kernel,
        [((COLS, 40, D), BF16), ((ROWS, TR, D), BF16), ((ROWS, TR, D), BF16)],
        from_rows,
        own,
        meta,
    )
    wide, side = call(
        params_kernel,
        [((16, D), F32), ((2, 4 * HEADS, LINE), F32)],
        first,
        norm_gain.reshape(1, D),
        out_gain.reshape(1, D),
        conv_weight,
        dt_bias,
        row_rate,
        col_rate,
        pinned=(0,),
    )
    ends = COLS - 1
    right = lax.ppermute(first, "col", [(i + 1, i) for i in range(ends)])
    left = lax.ppermute(last, "col", [(i, i + 1) for i in range(ends)])
    from_cols = lax.all_to_all(packed, "col", 0, 0, tiled=True)
    by_row, tokens = call(
        row_kernel,
        [((LINE, D), BF16), ((LINE, D), F32)],
        from_cols,
        wide,
        side,
        cond_weight,
        in_weight,
        bc_weight,
        dt_weight,
        scratch=[
            pltpu.VMEM((LINE, HEADS * LINE), BF16),
            pltpu.VMEM((HEADS * LINE, D), BF16),
        ],
    )
    by_row = lax.all_to_all(by_row.reshape(COLS, TC, D), "col", 0, 0, tiled=True)
    hidden, gate, by_column = call(
        column_kernel,
        [((LINE, D), F32), ((LINE, D), F32), ((LINE, D), F32)],
        from_rows,
        left,
        right,
        tokens,
        own,
        wide,
        side,
        in_weight,
        bc_weight,
        dt_weight,
        scratch=[
            pltpu.VMEM(((TC + 2) * LINE, D), BF16),
            pltpu.VMEM(((TC + 2) * LINE, D), BF16),
            pltpu.VMEM((TC * LINE, D), BF16),
            pltpu.VMEM((TC * LINE, 2 * STATE), BF16),
            pltpu.VMEM((2, LINE, LINE), F32),
            pltpu.VMEM((TC, HEADS * TR, LINE), BF16),
            pltpu.VMEM((LINE, D), F32),
        ],
    )
    (out,) = call(
        finish_kernel,
        [((TR, TC, D), BF16)],
        by_row,
        by_column,
        hidden,
        gate,
        wide,
        out_weight,
        result=True,
    )
    return out


def solution(mesh):
    placed = (
        P("row", "col", None),
        P(("row", "col"), None),
        P(),
        P("col"),
        P(),
        P(),
        P(),
        P(),
        P(),
        P(),
        P(),
        P(),
        P("row", "col"),
        P(),
        P(),
    )
    return jax.shard_map(
        per_device, mesh=mesh, in_specs=placed, out_specs=P("row", "col", None), check_vma=False
    )
```

```python
import jax
import jax.numpy as jnp
from jax import lax
from jax.experimental import pallas as pl
from jax.experimental.pallas import tpu as pltpu
from jax.sharding import PartitionSpec as P

F32 = jnp.float32
BF16 = jnp.bfloat16
ROWS = 8
COLS = 16
TR = 16
TC = 8
LINE = 128
D = 256
HEADS = 16
HEAD_DIM = 16
STATE = 128


def iota(shape, dim):
    return lax.broadcasted_iota(jnp.int32, shape, dim)


def halves(x):
    high = x.astype(BF16).astype(F32)
    return high, x - high


def silu(x):
    return x * jax.nn.sigmoid(x)


def pack_row_kernel(
    trace_ref,
    latent_ref,
    logs_ref,
    horizon_ref,
    gain_ref,
    last_ref,
    conv_ref,
    bias_ref,
    row_ref,
    col_ref,
    out_ref,
    meta_ref,
    own_ref,
    wide_ref,
    side_ref,
):
    r = lax.axis_index("row")
    c = lax.axis_index("col")
    own_ref[...] = latent_ref[...]
    target = iota((LINE, LINE), 0)
    source = iota((LINE, LINE), 1)
    pick = ((target & (TR - 1)) * TC + (target >> 4) == source).astype(BF16)
    flat = latent_ref[...].astype(F32).reshape(LINE, D).astype(BF16)
    columns = jnp.dot(pick, flat, preferred_element_type=F32).astype(BF16)
    high, low = halves(horizon_ref[...])
    place = iota((TR, LINE), 1)
    cell = iota((TR, LINE), 0)
    first = (place - TR * r == cell).astype(BF16)
    second = (place - ((TR * r + LINE // 2) & (LINE - 1)) == cell).astype(BF16)
    lines = jnp.dot(high.astype(BF16), first, preferred_element_type=F32) + jnp.dot(
        low.astype(BF16), second, preferred_element_type=F32
    )
    log = logs_ref[...].astype(F32)
    row8 = iota((8, LINE), 0)
    log = jnp.where(
        row8 == 0,
        jnp.broadcast_to(log[:, :LINE], (8, LINE)),
        jnp.broadcast_to(log[:, LINE:], (8, LINE)),
    )
    extra = jnp.concatenate([lines, log], axis=0).astype(BF16)
    for dest in range(ROWS):
        for j in range(TC):
            out_ref[dest, :, j * D : (j + 1) * D] = columns[j * TR : (j + 1) * TR, :]
        out_ref[dest, :, TC * D :] = extra
    lane = iota((TR, LINE), 1) - TC * c
    lane1 = iota((1, LINE), 1) - TC * c
    spread = jnp.zeros((TR, LINE), F32)
    trace = jnp.zeros((1, LINE), F32)
    across = horizon_ref[...].T
    for j in range(TC):
        column = jnp.broadcast_to(across[:, j : j + 1], (TR, LINE))
        spread = jnp.where(lane == j, column, spread)
        trace = jnp.where(lane1 == j, trace_ref[j].astype(F32), trace)
    high, low = halves(spread)
    row8 = iota((8, LINE), 0)
    for dest in range(COLS):
        part = jnp.where(row8 == 0, jnp.broadcast_to(trace, (8, LINE)), 0.0)
        part = jnp.where(row8 == 1, jnp.broadcast_to(high[dest : dest + 1], (8, LINE)), part)
        part = jnp.where(row8 == 2, jnp.broadcast_to(low[dest : dest + 1], (8, LINE)), part)
        meta_ref[dest] = part.astype(BF16)
    wide_ref[0:9, :] = conv_ref[...]
    wide_ref[9:10, :] = gain_ref[...]
    wide_ref[10:11, :] = last_ref[...]
    bias = bias_ref[...].T
    rates = [row_ref[...].T / 2048.0, col_ref[...].T / 2048.0]
    for k in range(4):
        side_ref[0, k * HEADS : (k + 1) * HEADS, :] = jnp.broadcast_to(
            bias[:, k : k + 1], (HEADS, LINE)
        )
        side_ref[1, k * HEADS : (k + 1) * HEADS, :] = jnp.broadcast_to(
            rates[k // 2][:, k % 2 : k % 2 + 1], (HEADS, LINE)
        )


def pack_col_kernel(got_ref, own_ref, meta_ref, out_ref, left_ref, right_ref):
    r = lax.axis_index("row")
    up = got_ref[jnp.maximum(r - 1, 0)].astype(F32)[TR - 1 : TR, :]
    down = got_ref[jnp.minimum(r + 1, ROWS - 1)].astype(F32)[0:1, :]
    above = jnp.concatenate([up[:, j * D : (j + 1) * D] for j in range(TC)], axis=0)
    below = jnp.concatenate([down[:, j * D : (j + 1) * D] for j in range(TC)], axis=0)
    own = own_ref[...].astype(F32)
    extra = got_ref[:, :, TC * D :].astype(F32)
    logs = jnp.concatenate(
        [
            jnp.concatenate([extra[s, 8 + half : 9 + half, :] for s in range(ROWS)], axis=0)
            for half in range(2)
        ],
        axis=1,
    )
    rows = [above] + [own[i] for i in range(TR)] + [below]
    rows = [x.astype(BF16) for x in rows]
    logs = logs.astype(BF16)
    for dest in range(COLS):
        for slot in range(3):
            out_ref[dest, :, slot * D : (slot + 1) * D] = rows[dest + slot]
        out_ref[dest, :, 3 * D : 4 * D] = logs
        out_ref[dest, :, 4 * D :] = meta_ref[dest]
    left_ref[...] = got_ref[:, :, 0:D]
    right_ref[...] = got_ref[:, :, (TC - 1) * D : TC * D]


def normalised(hidden, gain):
    scale = lax.rsqrt(jnp.mean(hidden * hidden, axis=-1, keepdims=True) + 1e-06)
    return (hidden * scale * gain).astype(BF16)


def line_scan(cells, tokens, inside, taps, gain, in_w, bc, dt_w, bias, rate, horizon, w_ref, x_ref):
    n = jnp.concatenate([normalised(cells[s] + tokens[s], gain) for s in range(3)], axis=0)
    p = jnp.dot(n, in_w, preferred_element_type=F32).astype(BF16).astype(F32)
    pre = [
        jnp.where(inside[s], p[s * LINE : (s + 1) * LINE, :], 0.0) for s in range(3)
    ]
    shifted = [
        taps[t][0] * pre[0] + taps[t][1] * pre[1] + taps[t][2] * pre[2] for t in range(3)
    ]
    place = iota((LINE, D), 0)
    conv = (
        shifted[1]
        + jnp.where(place == 0, 0.0, pltpu.roll(shifted[0], 1, 0))
        + jnp.where(place == LINE - 1, 0.0, pltpu.roll(shifted[2], LINE - 1, 0))
    )
    mixed = silu(conv).astype(BF16)
    coef = jnp.dot(mixed, bc, preferred_element_type=F32).astype(BF16)
    contract = (((1,), (1,)), ((), ()))
    k = iota((LINE, LINE), 0)
    j = iota((LINE, LINE), 1)
    lower = j <= k
    score_f = lax.dot_general(
        coef[:, STATE : 2 * STATE], coef[:, :STATE], contract, preferred_element_type=F32
    )
    score_b = lax.dot_general(
        coef[:, 3 * STATE :], coef[:, 2 * STATE : 3 * STATE], contract, preferred_element_type=F32
    )
    score_f = jnp.where(lower, score_f, 0.0)
    score_b = jnp.where(j >= k, score_b, 0.0)
    z = lax.dot_general(dt_w, mixed, contract, preferred_element_type=F32) + bias
    step = jnp.maximum(z, 0.0) + jnp.log1p(jnp.exp(-jnp.abs(z)))
    decay = -step * rate - horizon
    high, rest = halves(decay)
    middle, low = halves(rest)
    steps = []
    sums_t = []
    for side in range(2):
        at = slice(side * HEADS, (side + 1) * HEADS)
        steps.append(step[at])
        ones = ((k <= j) if side == 0 else (k >= j)).astype(BF16)
        parts = jnp.concatenate([high[at], middle[at], low[at]], axis=0).astype(BF16)
        total = jnp.dot(parts, ones, preferred_element_type=F32)
        total = total[:HEADS] + (total[HEADS : 2 * HEADS] + total[2 * HEADS :])
        sums_t.append(total)
    sums = [x.T for x in sums_t]
    head_of = iota((LINE, D), 1) // HEAD_DIM
    wide = mixed.astype(F32)
    for h in range(HEADS):
        ahead = sums[0][:, h : h + 1] - sums_t[0][h : h + 1, :]
        behind = sums[1][:, h : h + 1] - sums_t[1][h : h + 1, :]
        decay = jnp.exp(jnp.where(lower, ahead, behind))
        drive = score_f * steps[0][h : h + 1, :] + score_b * steps[1][h : h + 1, :]
        w_ref[:, h * LINE : (h + 1) * LINE] = (drive * decay).astype(BF16)
        x_ref[h * LINE : (h + 1) * LINE, :] = jnp.where(head_of == h, wide, 0.0).astype(BF16)
    return jnp.dot(w_ref[...], x_ref[...], preferred_element_type=F32)


def row_kernel(
    cols_ref,
    wide_ref,
    side_ref,
    cond_ref,
    in_ref,
    bc_ref,
    dt_ref,
    out_ref,
    tokens_ref,
    w_ref,
    x_ref,
):
    r = lax.axis_index("row")
    c = lax.axis_index("col")
    logs = cols_ref[:, :, 3 * D : 4 * D].astype(F32).reshape(LINE, D).astype(BF16)
    tokens = silu(jnp.dot(logs, cond_ref[...], preferred_element_type=F32)).astype(BF16)
    meta = jnp.sum(cols_ref[:, :, 4 * D :].astype(F32), axis=0)
    trace = jnp.broadcast_to(meta[0:1, :], (8, LINE)).T[:, 0:1].astype(jnp.int32)
    position = iota((1, LINE), 1)
    names = (position & (ROWS - 1)) * COLS + (position >> 3)
    chosen = (names == trace).astype(BF16)
    tokens = jnp.dot(chosen, tokens, preferred_element_type=F32)
    tokens_ref[...] = tokens
    row = r * TR + c
    cells = [
        cols_ref[:, :, s * D : (s + 1) * D].astype(F32).reshape(LINE, D) for s in range(3)
    ]
    out_ref[...] = line_scan(
        cells,
        [tokens, tokens, tokens],
        [row > 0, True, row < LINE - 1],
        [[wide_ref[3 * s + t : 3 * s + t + 1, :] for s in range(3)] for t in range(3)],
        wide_ref[9:10, :],
        in_ref[:, :D],
        bc_ref[:, : 4 * STATE],
        dt_ref[: 2 * HEADS, :],
        side_ref[0, : 2 * HEADS, :],
        side_ref[1, : 2 * HEADS, :],
        meta[1:2, :] + meta[2:3, :],
        w_ref,
        x_ref,
    ).astype(BF16)


def column_kernel(
    rows_ref,
    left_ref,
    right_ref,
    tokens_ref,
    own_ref,
    wide_ref,
    side_ref,
    in_ref,
    bc_ref,
    dt_ref,
    hidden_ref,
    gate_ref,
    sum_ref,
    normed_ref,
    pre_ref,
    mixed_ref,
    b_ref,
    cum_ref,
    w_ref,
    y_ref,
):
    r = lax.axis_index("row")
    c = lax.axis_index("col")
    gain = wide_ref[9:10, :]
    hidden = own_ref[...].astype(F32) + tokens_ref[pl.ds(pl.multiple_of(c * TC, TC), TC), :][None]
    hidden = hidden.reshape(LINE, D)
    hidden_ref[...] = hidden
    gate = jnp.dot(normalised(hidden, gain), in_ref[:, D:], preferred_element_type=F32)
    gate_ref[...] = silu(gate.astype(BF16).astype(F32))
    for q in range(TC + 2):
        if q == 0:
            cells = left_ref[...]
        elif q == TC + 1:
            cells = right_ref[...]
        else:
            cells = rows_ref[:, :, (q - 1) * D : q * D]
        line = jnp.clip(c * TC + q - 1, 0, LINE - 1)
        cells = cells.astype(F32).reshape(LINE, D) + tokens_ref[pl.ds(line, 1), :]
        normed_ref[q * LINE : (q + 1) * LINE, :] = normalised(cells, gain)
    pre_ref[...] = jnp.dot(
        normed_ref[...], in_ref[:, :D], preferred_element_type=F32
    ).astype(BF16)
    place = iota((LINE, D), 0)
    inside = [c > 0] + [True] * TC + [c < COLS - 1]
    for j in range(TC):
        pre = []
        for s in range(3):
            p = pre_ref[(j + s) * LINE : (j + s + 1) * LINE, :].astype(F32)
            pre.append(p if inside[j + s] is True else jnp.where(inside[j + s], p, 0.0))
        shifted = [
            sum(wide_ref[3 * a + s : 3 * a + s + 1, :] * pre[s] for s in range(3))
            for a in range(3)
        ]
        conv = (
            shifted[1]
            + jnp.where(place == 0, 0.0, pltpu.roll(shifted[0], 1, 0))
            + jnp.where(place == LINE - 1, 0.0, pltpu.roll(shifted[2], LINE - 1, 0))
        )
        mixed_ref[j * LINE : (j + 1) * LINE, :] = silu(conv).astype(BF16)
    base = 4 * STATE
    b_weight = jnp.concatenate(
        [bc_ref[:, base : base + STATE], bc_ref[:, base + 2 * STATE : base + 3 * STATE]], axis=1
    )
    c_weight = jnp.concatenate(
        [bc_ref[:, base + STATE : base + 2 * STATE], bc_ref[:, base + 3 * STATE :]], axis=1
    )
    b_ref[...] = jnp.dot(mixed_ref[...], b_weight, preferred_element_type=F32).astype(BF16)
    start = pl.multiple_of(r * TR, TR)
    mine = jnp.concatenate(
        [mixed_ref[pl.ds(j * LINE + start, TR), :] for j in range(TC)], axis=0
    )
    c_own = jnp.dot(mine, c_weight, preferred_element_type=F32).astype(BF16)
    contract = (((1,), (1,)), ((), ()))
    z = lax.dot_general(
        dt_ref[2 * HEADS :, :], mixed_ref[...], contract, preferred_element_type=F32
    )
    k = iota((LINE, LINE), 0)
    j_ = iota((LINE, LINE), 1)
    extra = rows_ref[:, :, TC * D :].astype(F32)
    owner = iota((TC, LINE), 1) >> 4
    high = jnp.zeros((TC, LINE), F32)
    low = jnp.zeros((TC, LINE), F32)
    for s in range(ROWS):
        high = jnp.where(owner == s, extra[s, :TC, :], high)
        low = jnp.where(owner == (s + ROWS // 2) % ROWS, extra[s, :TC, :], low)
    horizon = high + pltpu.roll(low, LINE // 2, 1)
    steps = []
    sums = []
    for side in range(2):
        bias = side_ref[0, (2 + side) * HEADS : (3 + side) * HEADS, :]
        rate = side_ref[1, (2 + side) * HEADS : (3 + side) * HEADS, :]
        own_steps = []
        decays = []
        for j in range(TC):
            zj = z[side * HEADS : (side + 1) * HEADS, j * LINE : (j + 1) * LINE] + bias
            step = jnp.maximum(zj, 0.0) + jnp.log1p(jnp.exp(-jnp.abs(zj)))
            own_steps.append(step)
            decays.append(-step * rate - horizon[j : j + 1, :])
        decay = jnp.concatenate(decays, axis=0)
        ones = ((k <= j_) if side == 0 else (k >= j_)).astype(BF16)
        high, rest = halves(decay)
        middle, low = halves(rest)
        parts = jnp.concatenate([high, middle, low], axis=0).astype(BF16)
        total = jnp.dot(parts, ones, preferred_element_type=F32)
        total = total[:LINE] + (total[LINE : 2 * LINE] + total[2 * LINE :])
        cum_ref[side] = total.T
        steps.append(own_steps)
        sums.append(total)
    ahead_own = cum_ref[0, pl.ds(start, TR), :]
    behind_own = cum_ref[1, pl.ds(start, TR), :]
    at = iota((TR, LINE), 0) + start
    other = iota((TR, LINE), 1)
    lower = other <= at
    upper = other >= at
    head_of = iota((TR, D), 1) // HEAD_DIM
    for j in range(TC):
        cj = c_own[j * TR : (j + 1) * TR, :]
        bj = b_ref[j * LINE : (j + 1) * LINE, :]
        score_f = lax.dot_general(
            cj[:, :STATE], bj[:, :STATE], contract, preferred_element_type=F32
        )
        score_b = lax.dot_general(
            cj[:, STATE:], bj[:, STATE:], contract, preferred_element_type=F32
        )
        score_f = jnp.where(lower, score_f, 0.0)
        score_b = jnp.where(upper, score_b, 0.0)
        for h in range(HEADS):
            n = j * HEADS + h
            ahead = ahead_own[:, n : n + 1] - sums[0][n : n + 1, :]
            behind = behind_own[:, n : n + 1] - sums[1][n : n + 1, :]
            decay = jnp.exp(jnp.where(lower, ahead, behind))
            drive = score_f * steps[0][j][h : h + 1, :] + score_b * steps[1][j][h : h + 1, :]
            w_ref[j, h * TR : (h + 1) * TR, :] = (drive * decay).astype(BF16)
        full = jnp.dot(
            w_ref[j], mixed_ref[j * LINE : (j + 1) * LINE, :], preferred_element_type=F32
        )
        got = full[:TR, :]
        for h in range(1, HEADS):
            got = jnp.where(head_of == h, full[h * TR : (h + 1) * TR, :], got)
        y_ref[j * TR : (j + 1) * TR, :] = got
    pick = ((k % TC) * TR + k // TC == j_).astype(BF16)
    high, low = halves(y_ref[...])
    sum_ref[...] = jnp.dot(pick, high.astype(BF16), preferred_element_type=F32) + jnp.dot(
        pick, low.astype(BF16), preferred_element_type=F32
    )


def finish_kernel(row_ref, col_ref, hidden_ref, gate_ref, wide_ref, out_w_ref, out_ref):
    total = row_ref[...].astype(F32).reshape(LINE, D) + col_ref[...]
    scale = lax.rsqrt(jnp.mean(total * total, axis=-1, keepdims=True) + 1e-05)
    gated = (total * scale * wide_ref[10:11, :] * gate_ref[...]).astype(BF16)
    branch = jnp.dot(gated, out_w_ref[...], preferred_element_type=F32)
    out_ref[...] = (hidden_ref[...] + branch).reshape(TR, TC, D).astype(BF16)


def call(kernel, outs, *args, scratch=(), smem=0, pinned=True, result=False):
    vmem = pl.BlockSpec(memory_space=pltpu.VMEM)
    specs = [pl.BlockSpec(memory_space=pltpu.SMEM)] * smem + [vmem] * (len(args) - smem)
    if pinned is True:
        pinned = range(smem, len(args))
    args = [
        pltpu.with_memory_space_constraint(x, pltpu.VMEM) if i in pinned else x
        for i, x in enumerate(args)
    ]
    shape = jax.ShapeDtypeStruct if result else pltpu.VMEM
    return pl.pallas_call(
        kernel,
        out_shape=[shape(s, d) for s, d in outs],
        in_specs=specs,
        out_specs=[vmem] * len(outs),
        scratch_shapes=list(scratch),
        name=kernel.__name__,
    )(*args)


def per_device(
    latent,
    well_logs,
    cond_weight,
    trace_rows,
    norm_gain,
    in_weight,
    conv_weight,
    bc_weight,
    dt_weight,
    dt_bias,
    row_rate,
    col_rate,
    horizon,
    out_gain,
    out_weight,
):
    dt_weight = dt_weight.T
    packed, meta, own, wide, side = call(
        pack_row_kernel,
        [
            ((ROWS, TR, TC * D + LINE), BF16),
            ((COLS, 8, LINE), BF16),
            ((TR, TC, D), BF16),
            ((16, D), F32),
            ((2, 4 * HEADS, LINE), F32),
        ],
        trace_rows,
        latent,
        well_logs,
        horizon.T,
        norm_gain.reshape(1, D),
        out_gain.reshape(1, D),
        conv_weight,
        dt_bias,
        row_rate,
        col_rate,
        smem=1,
        pinned=(),
    )
    from_rows = lax.all_to_all(packed, "row", 0, 0, tiled=True)
    packed, first, last = call(
        pack_col_kernel,
        [((COLS, 8, 4 * D + LINE), BF16), ((ROWS, TR, D), BF16), ((ROWS, TR, D), BF16)],
        from_rows,
        own,
        meta,
    )
    ends = COLS - 1
    right = lax.ppermute(first, "col", [(i + 1, i) for i in range(ends)])
    left = lax.ppermute(last, "col", [(i, i + 1) for i in range(ends)])
    from_cols = lax.all_to_all(packed, "col", 0, 0, tiled=True)
    by_row, tokens = call(
        row_kernel,
        [((LINE, D), BF16), ((LINE, D), F32)],
        from_cols,
        wide,
        side,
        cond_weight,
        in_weight,
        bc_weight,
        dt_weight,
        scratch=[
            pltpu.VMEM((LINE, HEADS * LINE), BF16),
            pltpu.VMEM((HEADS * LINE, D), BF16),
        ],
    )
    by_row = lax.all_to_all(by_row.reshape(COLS, TC, D), "col", 0, 0, tiled=True)
    hidden, gate, by_column = call(
        column_kernel,
        [((LINE, D), F32), ((LINE, D), F32), ((LINE, D), F32)],
        from_rows,
        left,
        right,
        tokens,
        own,
        wide,
        side,
        in_weight,
        bc_weight,
        dt_weight,
        scratch=[
            pltpu.VMEM(((TC + 2) * LINE, D), BF16),
            pltpu.VMEM(((TC + 2) * LINE, D), BF16),
            pltpu.VMEM((TC * LINE, D), BF16),
            pltpu.VMEM((TC * LINE, 2 * STATE), BF16),
            pltpu.VMEM((2, LINE, LINE), F32),
            pltpu.VMEM((TC, HEADS * TR, LINE), BF16),
            pltpu.VMEM((LINE, D), F32),
        ],
    )
    (out,) = call(
        finish_kernel,
        [((TR, TC, D), BF16)],
        by_row,
        by_column,
        hidden,
        gate,
        wide,
        out_weight,
        result=True,
    )
    return out


def solution(mesh):
    placed = (
        P("row", "col", None),
        P(("row", "col"), None),
        P(),
        P("col"),
        P(),
        P(),
        P(),
        P(),
        P(),
        P(),
        P(),
        P(),
        P("row", "col"),
        P(),
        P(),
    )
    return jax.shard_map(
        per_device, mesh=mesh, in_specs=placed, out_specs=P("row", "col", None), check_vma=False
    )
```

```python
import jax
import jax.numpy as jnp
from jax import lax
from jax.experimental import pallas as pl
from jax.experimental.pallas import tpu as pltpu
from jax.sharding import PartitionSpec as P

F32 = jnp.float32
BF16 = jnp.bfloat16
ROWS = 8
COLS = 16
TR = 16
TC = 8
LINE = 128
D = 256
HEADS = 16
HEAD_DIM = 16
STATE = 128
ROW_ORDER = (5, 7, 3, 1, 4, 6, 2, 0)
COL_ORDER = (15, 14, 13, 12, 11, 10, 9, 8, 7, 6, 5, 4, 3, 2, 1, 0)
ROW_PLACE = tuple(ROW_ORDER.index(i) for i in range(ROWS))
MID_ORDER = (15, 14, 13, 12, 11, 10, 9, 8, 7, 6, 5, 4, 3, 2, 1, 0)
MID_PLACE = tuple(MID_ORDER.index(i) for i in range(COLS))
COL_PLACE = tuple(COL_ORDER.index(i) for i in range(COLS))


def iota(shape, dim):
    return lax.broadcasted_iota(jnp.int32, shape, dim)


def place_of(row):
    return sum(jnp.where(row == i, ROW_PLACE[i], 0) for i in range(ROWS))


def halves(x):
    high = x.astype(BF16).astype(F32)
    return high, x - high


def silu(x):
    return x * jax.nn.sigmoid(x)


def pack_row_kernel(
    trace_ref,
    latent_ref,
    logs_ref,
    horizon_ref,
    gain_ref,
    last_ref,
    conv_ref,
    bias_ref,
    row_ref,
    col_ref,
    out_ref,
    meta_ref,
    own_ref,
    wide_ref,
    side_ref,
):
    r = lax.axis_index("row")
    c = lax.axis_index("col")
    own_ref[...] = latent_ref[...]
    target = iota((LINE, LINE), 0)
    source = iota((LINE, LINE), 1)
    pick = ((target & (TR - 1)) * TC + (target >> 4) == source).astype(BF16)
    flat = latent_ref[...].astype(F32).reshape(LINE, D).astype(BF16)
    columns = jnp.dot(pick, flat, preferred_element_type=F32).astype(BF16)
    high, low = halves(horizon_ref[...])
    place = iota((TR, LINE), 1)
    cell = iota((TR, LINE), 0)
    first = (place - TR * r == cell).astype(BF16)
    second = (place - ((TR * r + LINE // 2) & (LINE - 1)) == cell).astype(BF16)
    lines = jnp.dot(high.astype(BF16), first, preferred_element_type=F32) + jnp.dot(
        low.astype(BF16), second, preferred_element_type=F32
    )
    log = logs_ref[...].astype(F32)
    row8 = iota((8, LINE), 0)
    log = jnp.where(
        row8 == 0,
        jnp.broadcast_to(log[:, :LINE], (8, LINE)),
        jnp.broadcast_to(log[:, LINE:], (8, LINE)),
    )
    extra = jnp.concatenate([lines, log], axis=0).astype(BF16)
    for dest in range(ROWS):
        for j in range(TC):
            out_ref[dest, :, j * D : (j + 1) * D] = columns[j * TR : (j + 1) * TR, :]
        out_ref[dest, :, TC * D :] = extra
    lane = iota((TR, LINE), 1) - TC * c
    lane1 = iota((1, LINE), 1) - TC * c
    spread = jnp.zeros((TR, LINE), F32)
    trace = jnp.zeros((1, LINE), F32)
    across = horizon_ref[...].T
    for j in range(TC):
        column = jnp.broadcast_to(across[:, j : j + 1], (TR, LINE))
        spread = jnp.where(lane == j, column, spread)
        trace = jnp.where(lane1 == j, trace_ref[j].astype(F32), trace)
    high, low = halves(spread)
    row8 = iota((8, LINE), 0)
    for dest in range(COLS):
        part = jnp.where(row8 == 0, jnp.broadcast_to(trace, (8, LINE)), 0.0)
        part = jnp.where(row8 == 1, jnp.broadcast_to(high[dest : dest + 1], (8, LINE)), part)
        part = jnp.where(row8 == 2, jnp.broadcast_to(low[dest : dest + 1], (8, LINE)), part)
        meta_ref[dest] = part.astype(BF16)
    wide_ref[0:9, :] = conv_ref[...]
    wide_ref[9:10, :] = gain_ref[...]
    wide_ref[10:11, :] = last_ref[...]
    bias = bias_ref[...].T
    rates = [row_ref[...].T / 2048.0, col_ref[...].T / 2048.0]
    for k in range(4):
        side_ref[0, k * HEADS : (k + 1) * HEADS, :] = jnp.broadcast_to(
            bias[:, k : k + 1], (HEADS, LINE)
        )
        side_ref[1, k * HEADS : (k + 1) * HEADS, :] = jnp.broadcast_to(
            rates[k // 2][:, k % 2 : k % 2 + 1], (HEADS, LINE)
        )


def pack_col_kernel(got_ref, own_ref, meta_ref, out_ref, left_ref, right_ref):
    r = lax.axis_index("row")
    up = got_ref[place_of(jnp.maximum(r - 1, 0))].astype(F32)[TR - 1 : TR, :]
    down = got_ref[place_of(jnp.minimum(r + 1, ROWS - 1))].astype(F32)[0:1, :]
    above = jnp.concatenate([up[:, j * D : (j + 1) * D] for j in range(TC)], axis=0)
    below = jnp.concatenate([down[:, j * D : (j + 1) * D] for j in range(TC)], axis=0)
    own = own_ref[...].astype(F32)
    extra = got_ref[:, :, TC * D :].astype(F32)
    logs = jnp.concatenate(
        [
            jnp.concatenate([extra[s, 8 + half : 9 + half, :] for s in ROW_PLACE], axis=0)
            for half in range(2)
        ],
        axis=1,
    )
    rows = [above] + [own[i] for i in range(TR)] + [below]
    rows = [x.astype(BF16) for x in rows]
    logs = logs.astype(BF16)
    for dest, place in enumerate(MID_PLACE):
        for slot in range(3):
            out_ref[place, :, slot * D : (slot + 1) * D] = rows[dest + slot]
        out_ref[place, :, 3 * D : 4 * D] = logs
        out_ref[place, :, 4 * D :] = meta_ref[dest]
    for i, s in enumerate(ROW_PLACE):
        left_ref[i] = got_ref[s, :, 0:D]
        right_ref[i] = got_ref[s, :, (TC - 1) * D : TC * D]


def normalised(hidden, gain):
    scale = lax.rsqrt(jnp.mean(hidden * hidden, axis=-1, keepdims=True) + 1e-06)
    return (hidden * scale * gain).astype(BF16)


def line_scan(cells, tokens, inside, taps, gain, in_w, bc, dt_w, bias, rate, horizon, w_ref, x_ref):
    n = jnp.concatenate([normalised(cells[s] + tokens[s], gain) for s in range(3)], axis=0)
    p = jnp.dot(n, in_w, preferred_element_type=F32).astype(BF16).astype(F32)
    pre = [
        jnp.where(inside[s], p[s * LINE : (s + 1) * LINE, :], 0.0) for s in range(3)
    ]
    shifted = [
        taps[t][0] * pre[0] + taps[t][1] * pre[1] + taps[t][2] * pre[2] for t in range(3)
    ]
    place = iota((LINE, D), 0)
    conv = (
        shifted[1]
        + jnp.where(place == 0, 0.0, pltpu.roll(shifted[0], 1, 0))
        + jnp.where(place == LINE - 1, 0.0, pltpu.roll(shifted[2], LINE - 1, 0))
    )
    mixed = silu(conv).astype(BF16)
    coef = jnp.dot(mixed, bc, preferred_element_type=F32).astype(BF16)
    contract = (((1,), (1,)), ((), ()))
    k = iota((LINE, LINE), 0)
    j = iota((LINE, LINE), 1)
    lower = j <= k
    score_f = lax.dot_general(
        coef[:, STATE : 2 * STATE], coef[:, :STATE], contract, preferred_element_type=F32
    )
    score_b = lax.dot_general(
        coef[:, 3 * STATE :], coef[:, 2 * STATE : 3 * STATE], contract, preferred_element_type=F32
    )
    score_f = jnp.where(lower, score_f, 0.0)
    score_b = jnp.where(j >= k, score_b, 0.0)
    z = lax.dot_general(dt_w, mixed, contract, preferred_element_type=F32) + bias
    step = jnp.maximum(z, 0.0) + jnp.log1p(jnp.exp(-jnp.abs(z)))
    decay = -step * rate - horizon
    high, rest = halves(decay)
    middle, low = halves(rest)
    steps = []
    sums_t = []
    for side in range(2):
        at = slice(side * HEADS, (side + 1) * HEADS)
        steps.append(step[at])
        ones = ((k <= j) if side == 0 else (k >= j)).astype(BF16)
        parts = jnp.concatenate([high[at], middle[at], low[at]], axis=0).astype(BF16)
        total = jnp.dot(parts, ones, preferred_element_type=F32)
        total = total[:HEADS] + (total[HEADS : 2 * HEADS] + total[2 * HEADS :])
        sums_t.append(total)
    sums = [x.T for x in sums_t]
    head_of = iota((LINE, D), 1) // HEAD_DIM
    wide = mixed.astype(F32)
    for h in range(HEADS):
        ahead = sums[0][:, h : h + 1] - sums_t[0][h : h + 1, :]
        behind = sums[1][:, h : h + 1] - sums_t[1][h : h + 1, :]
        decay = jnp.exp(jnp.where(lower, ahead, behind))
        drive = score_f * steps[0][h : h + 1, :] + score_b * steps[1][h : h + 1, :]
        w_ref[:, h * LINE : (h + 1) * LINE] = (drive * decay).astype(BF16)
        x_ref[h * LINE : (h + 1) * LINE, :] = jnp.where(head_of == h, wide, 0.0).astype(BF16)
    return jnp.dot(w_ref[...], x_ref[...], preferred_element_type=F32)


def row_kernel(
    cols_ref,
    wide_ref,
    side_ref,
    cond_ref,
    in_ref,
    bc_ref,
    dt_ref,
    out_ref,
    tokens_ref,
    w_ref,
    x_ref,
):
    r = lax.axis_index("row")
    c = lax.axis_index("col")
    logs, *cells = [
        jnp.stack([cols_ref[p, :, s * D : (s + 1) * D] for p in MID_PLACE])
        .astype(F32)
        .reshape(LINE, D)
        for s in (3, 0, 1, 2)
    ]
    logs = logs.astype(BF16)
    tokens = silu(jnp.dot(logs, cond_ref[...], preferred_element_type=F32)).astype(BF16)
    meta = jnp.sum(cols_ref[:, :, 4 * D :].astype(F32), axis=0)
    trace = jnp.broadcast_to(meta[0:1, :], (8, LINE)).T[:, 0:1].astype(jnp.int32)
    position = iota((1, LINE), 1)
    names = (position & (ROWS - 1)) * COLS + (position >> 3)
    chosen = (names == trace).astype(BF16)
    tokens = jnp.dot(chosen, tokens, preferred_element_type=F32)
    tokens_ref[...] = tokens
    row = r * TR + c
    scanned = line_scan(
        cells,
        [tokens, tokens, tokens],
        [row > 0, True, row < LINE - 1],
        [[wide_ref[3 * s + t : 3 * s + t + 1, :] for s in range(3)] for t in range(3)],
        wide_ref[9:10, :],
        in_ref[:, :D],
        bc_ref[:, : 4 * STATE],
        dt_ref[: 2 * HEADS, :],
        side_ref[0, : 2 * HEADS, :],
        side_ref[1, : 2 * HEADS, :],
        meta[1:2, :] + meta[2:3, :],
        w_ref,
        x_ref,
    )
    out_ref[...] = jnp.concatenate(
        [scanned[i * TC : (i + 1) * TC, :] for i in COL_ORDER], axis=0
    ).astype(BF16)


def column_kernel(
    rows_ref,
    left_ref,
    right_ref,
    tokens_ref,
    own_ref,
    wide_ref,
    side_ref,
    in_ref,
    bc_ref,
    dt_ref,
    hidden_ref,
    gate_ref,
    sum_ref,
    normed_ref,
    pre_ref,
    mixed_ref,
    b_ref,
    cum_ref,
    w_ref,
    y_ref,
):
    r = lax.axis_index("row")
    c = lax.axis_index("col")
    gain = wide_ref[9:10, :]
    hidden = own_ref[...].astype(F32) + tokens_ref[pl.ds(pl.multiple_of(c * TC, TC), TC), :][None]
    hidden = hidden.reshape(LINE, D)
    hidden_ref[...] = hidden
    gate = jnp.dot(normalised(hidden, gain), in_ref[:, D:], preferred_element_type=F32)
    gate_ref[...] = silu(gate.astype(BF16).astype(F32))
    for q in range(TC + 2):
        if q == 0:
            cells = left_ref[...]
        elif q == TC + 1:
            cells = right_ref[...]
        else:
            cells = jnp.stack([rows_ref[s, :, (q - 1) * D : q * D] for s in ROW_PLACE])
        line = jnp.clip(c * TC + q - 1, 0, LINE - 1)
        cells = cells.astype(F32).reshape(LINE, D) + tokens_ref[pl.ds(line, 1), :]
        normed_ref[q * LINE : (q + 1) * LINE, :] = normalised(cells, gain)
    pre_ref[...] = jnp.dot(
        normed_ref[...], in_ref[:, :D], preferred_element_type=F32
    ).astype(BF16)
    place = iota((LINE, D), 0)
    inside = [c > 0] + [True] * TC + [c < COLS - 1]
    for j in range(TC):
        pre = []
        for s in range(3):
            p = pre_ref[(j + s) * LINE : (j + s + 1) * LINE, :].astype(F32)
            pre.append(p if inside[j + s] is True else jnp.where(inside[j + s], p, 0.0))
        shifted = [
            sum(wide_ref[3 * a + s : 3 * a + s + 1, :] * pre[s] for s in range(3))
            for a in range(3)
        ]
        conv = (
            shifted[1]
            + jnp.where(place == 0, 0.0, pltpu.roll(shifted[0], 1, 0))
            + jnp.where(place == LINE - 1, 0.0, pltpu.roll(shifted[2], LINE - 1, 0))
        )
        mixed_ref[j * LINE : (j + 1) * LINE, :] = silu(conv).astype(BF16)
    base = 4 * STATE
    b_weight = jnp.concatenate(
        [bc_ref[:, base : base + STATE], bc_ref[:, base + 2 * STATE : base + 3 * STATE]], axis=1
    )
    c_weight = jnp.concatenate(
        [bc_ref[:, base + STATE : base + 2 * STATE], bc_ref[:, base + 3 * STATE :]], axis=1
    )
    b_ref[...] = jnp.dot(mixed_ref[...], b_weight, preferred_element_type=F32).astype(BF16)
    start = pl.multiple_of(r * TR, TR)
    mine = jnp.concatenate(
        [mixed_ref[pl.ds(j * LINE + start, TR), :] for j in range(TC)], axis=0
    )
    c_own = jnp.dot(mine, c_weight, preferred_element_type=F32).astype(BF16)
    contract = (((1,), (1,)), ((), ()))
    z = lax.dot_general(
        dt_ref[2 * HEADS :, :], mixed_ref[...], contract, preferred_element_type=F32
    )
    k = iota((LINE, LINE), 0)
    j_ = iota((LINE, LINE), 1)
    extra = rows_ref[:, :, TC * D :].astype(F32)
    owner = iota((TC, LINE), 1) >> 4
    high = jnp.zeros((TC, LINE), F32)
    low = jnp.zeros((TC, LINE), F32)
    for i, s in enumerate(ROW_PLACE):
        high = jnp.where(owner == i, extra[s, :TC, :], high)
        low = jnp.where(owner == (i + ROWS // 2) % ROWS, extra[s, :TC, :], low)
    horizon = high + pltpu.roll(low, LINE // 2, 1)
    steps = []
    sums = []
    for side in range(2):
        bias = side_ref[0, (2 + side) * HEADS : (3 + side) * HEADS, :]
        rate = side_ref[1, (2 + side) * HEADS : (3 + side) * HEADS, :]
        own_steps = []
        decays = []
        for j in range(TC):
            zj = z[side * HEADS : (side + 1) * HEADS, j * LINE : (j + 1) * LINE] + bias
            step = jnp.maximum(zj, 0.0) + jnp.log1p(jnp.exp(-jnp.abs(zj)))
            own_steps.append(step)
            decays.append(-step * rate - horizon[j : j + 1, :])
        decay = jnp.concatenate(decays, axis=0)
        ones = ((k <= j_) if side == 0 else (k >= j_)).astype(BF16)
        high, rest = halves(decay)
        middle, low = halves(rest)
        parts = jnp.concatenate([high, middle, low], axis=0).astype(BF16)
        total = jnp.dot(parts, ones, preferred_element_type=F32)
        total = total[:LINE] + (total[LINE : 2 * LINE] + total[2 * LINE :])
        cum_ref[side] = total.T
        steps.append(own_steps)
        sums.append(total)
    ahead_own = cum_ref[0, pl.ds(start, TR), :]
    behind_own = cum_ref[1, pl.ds(start, TR), :]
    at = iota((TR, LINE), 0) + start
    other = iota((TR, LINE), 1)
    lower = other <= at
    upper = other >= at
    head_of = iota((TR, D), 1) // HEAD_DIM
    for j in range(TC):
        cj = c_own[j * TR : (j + 1) * TR, :]
        bj = b_ref[j * LINE : (j + 1) * LINE, :]
        score_f = lax.dot_general(
            cj[:, :STATE], bj[:, :STATE], contract, preferred_element_type=F32
        )
        score_b = lax.dot_general(
            cj[:, STATE:], bj[:, STATE:], contract, preferred_element_type=F32
        )
        score_f = jnp.where(lower, score_f, 0.0)
        score_b = jnp.where(upper, score_b, 0.0)
        for h in range(HEADS):
            n = j * HEADS + h
            ahead = ahead_own[:, n : n + 1] - sums[0][n : n + 1, :]
            behind = behind_own[:, n : n + 1] - sums[1][n : n + 1, :]
            decay = jnp.exp(jnp.where(lower, ahead, behind))
            drive = score_f * steps[0][j][h : h + 1, :] + score_b * steps[1][j][h : h + 1, :]
            w_ref[j, h * TR : (h + 1) * TR, :] = (drive * decay).astype(BF16)
        full = jnp.dot(
            w_ref[j], mixed_ref[j * LINE : (j + 1) * LINE, :], preferred_element_type=F32
        )
        got = full[:TR, :]
        for h in range(1, HEADS):
            got = jnp.where(head_of == h, full[h * TR : (h + 1) * TR, :], got)
        y_ref[j * TR : (j + 1) * TR, :] = got
    pick = ((k % TC) * TR + k // TC == j_).astype(BF16)
    high, low = halves(y_ref[...])
    sum_ref[...] = jnp.dot(pick, high.astype(BF16), preferred_element_type=F32) + jnp.dot(
        pick, low.astype(BF16), preferred_element_type=F32
    )


def finish_kernel(row_ref, col_ref, hidden_ref, gate_ref, wide_ref, out_w_ref, out_ref):
    by_row = jnp.concatenate([row_ref[s].astype(F32) for s in COL_PLACE], axis=0)
    total = by_row + col_ref[...]
    scale = lax.rsqrt(jnp.mean(total * total, axis=-1, keepdims=True) + 1e-05)
    gated = (total * scale * wide_ref[10:11, :] * gate_ref[...]).astype(BF16)
    branch = jnp.dot(gated, out_w_ref[...], preferred_element_type=F32)
    out_ref[...] = (hidden_ref[...] + branch).reshape(TR, TC, D).astype(BF16)


def call(kernel, outs, *args, scratch=(), smem=0, pinned=True, result=False):
    vmem = pl.BlockSpec(memory_space=pltpu.VMEM)
    specs = [pl.BlockSpec(memory_space=pltpu.SMEM)] * smem + [vmem] * (len(args) - smem)
    if pinned is True:
        pinned = range(smem, len(args))
    args = [
        pltpu.with_memory_space_constraint(x, pltpu.VMEM) if i in pinned else x
        for i, x in enumerate(args)
    ]
    shape = jax.ShapeDtypeStruct if result else pltpu.VMEM
    return pl.pallas_call(
        kernel,
        out_shape=[shape(s, d) for s, d in outs],
        in_specs=specs,
        out_specs=[vmem] * len(outs),
        scratch_shapes=list(scratch),
        name=kernel.__name__,
    )(*args)


def per_device(
    latent,
    well_logs,
    cond_weight,
    trace_rows,
    norm_gain,
    in_weight,
    conv_weight,
    bc_weight,
    dt_weight,
    dt_bias,
    row_rate,
    col_rate,
    horizon,
    out_gain,
    out_weight,
):
    dt_weight = dt_weight.T
    packed, meta, own, wide, side = call(
        pack_row_kernel,
        [
            ((ROWS, TR, TC * D + LINE), BF16),
            ((COLS, 8, LINE), BF16),
            ((TR, TC, D), BF16),
            ((16, D), F32),
            ((2, 4 * HEADS, LINE), F32),
        ],
        trace_rows,
        latent,
        well_logs,
        horizon.T,
        norm_gain.reshape(1, D),
        out_gain.reshape(1, D),
        conv_weight,
        dt_bias,
        row_rate,
        col_rate,
        smem=1,
        pinned=(),
    )
    from_rows = lax.all_to_all(
        packed, "row", 0, 0, tiled=True, axis_index_groups=[list(ROW_ORDER)]
    )
    packed, first, last = call(
        pack_col_kernel,
        [((COLS, 8, 4 * D + LINE), BF16), ((ROWS, TR, D), BF16), ((ROWS, TR, D), BF16)],
        from_rows,
        own,
        meta,
    )
    ends = COLS - 1
    right = lax.ppermute(first, "col", [(i + 1, i) for i in range(ends)])
    left = lax.ppermute(last, "col", [(i, i + 1) for i in range(ends)])
    from_cols = lax.all_to_all(
        packed, "col", 0, 0, tiled=True, axis_index_groups=[list(MID_ORDER)]
    )
    by_row, tokens = call(
        row_kernel,
        [((LINE, D), BF16), ((LINE, D), F32)],
        from_cols,
        wide,
        side,
        cond_weight,
        in_weight,
        bc_weight,
        dt_weight,
        scratch=[
            pltpu.VMEM((LINE, HEADS * LINE), BF16),
            pltpu.VMEM((HEADS * LINE, D), BF16),
        ],
    )
    by_row = lax.all_to_all(
        by_row.reshape(COLS, TC, D), "col", 0, 0, tiled=True, axis_index_groups=[list(COL_ORDER)]
    )
    hidden, gate, by_column = call(
        column_kernel,
        [((LINE, D), F32), ((LINE, D), F32), ((LINE, D), F32)],
        from_rows,
        left,
        right,
        tokens,
        own,
        wide,
        side,
        in_weight,
        bc_weight,
        dt_weight,
        scratch=[
            pltpu.VMEM(((TC + 2) * LINE, D), BF16),
            pltpu.VMEM(((TC + 2) * LINE, D), BF16),
            pltpu.VMEM((TC * LINE, D), BF16),
            pltpu.VMEM((TC * LINE, 2 * STATE), BF16),
            pltpu.VMEM((2, LINE, LINE), F32),
            pltpu.VMEM((TC, HEADS * TR, LINE), BF16),
            pltpu.VMEM((LINE, D), F32),
        ],
    )
    (out,) = call(
        finish_kernel,
        [((TR, TC, D), BF16)],
        by_row,
        by_column,
        hidden,
        gate,
        wide,
        out_weight,
        result=True,
    )
    return out


def solution(mesh):
    placed = (
        P("row", "col", None),
        P(("row", "col"), None),
        P(),
        P("col"),
        P(),
        P(),
        P(),
        P(),
        P(),
        P(),
        P(),
        P(),
        P("row", "col"),
        P(),
        P(),
    )
    return jax.shard_map(
        per_device, mesh=mesh, in_specs=placed, out_specs=P("row", "col", None), check_vma=False
    )
```

```python
import jax
import jax.numpy as jnp
from jax import lax
from jax.experimental import pallas as pl
from jax.experimental.pallas import tpu as pltpu
from jax.sharding import PartitionSpec as P

F32 = jnp.float32
BF16 = jnp.bfloat16
ROWS = 8
COLS = 16
TR = 16
TC = 8
LINE = 128
D = 256
HEADS = 16
HEAD_DIM = 16
STATE = 128
ROW_ORDER = (5, 7, 3, 1, 4, 6, 2, 0)
COL_ORDER = (15, 14, 13, 12, 11, 10, 9, 8, 7, 6, 5, 4, 3, 2, 1, 0)
ROW_PLACE = tuple(ROW_ORDER.index(i) for i in range(ROWS))
MID_ORDER = (15, 14, 13, 12, 11, 10, 9, 8, 7, 6, 5, 4, 3, 2, 1, 0)
MID_PLACE = tuple(MID_ORDER.index(i) for i in range(COLS))
COL_PLACE = tuple(COL_ORDER.index(i) for i in range(COLS))


def iota(shape, dim):
    return lax.broadcasted_iota(jnp.int32, shape, dim)


def place_of(row):
    return sum(jnp.where(row == i, ROW_PLACE[i], 0) for i in range(ROWS))


def halves(x):
    high = x.astype(BF16).astype(F32)
    return high, x - high


def silu(x):
    return x * jax.nn.sigmoid(x)


def pack_row_kernel(
    trace_ref,
    latent_ref,
    logs_ref,
    horizon_ref,
    gain_ref,
    last_ref,
    conv_ref,
    bias_ref,
    row_ref,
    col_ref,
    out_ref,
    meta_ref,
    own_ref,
    wide_ref,
    side_ref,
):
    r = lax.axis_index("row")
    c = lax.axis_index("col")
    own_ref[...] = latent_ref[...]
    target = iota((LINE, LINE), 0)
    source = iota((LINE, LINE), 1)
    pick = ((target & (TR - 1)) * TC + (target >> 4) == source).astype(BF16)
    flat = latent_ref[...].astype(F32).reshape(LINE, D).astype(BF16)
    columns = jnp.dot(pick, flat, preferred_element_type=F32).astype(BF16)
    high, low = halves(horizon_ref[...])
    place = iota((TR, LINE), 1)
    cell = iota((TR, LINE), 0)
    first = (place - TR * r == cell).astype(BF16)
    second = (place - ((TR * r + LINE // 2) & (LINE - 1)) == cell).astype(BF16)
    lines = jnp.dot(high.astype(BF16), first, preferred_element_type=F32) + jnp.dot(
        low.astype(BF16), second, preferred_element_type=F32
    )
    log = logs_ref[...].astype(F32)
    row8 = iota((8, LINE), 0)
    log = jnp.where(
        row8 == 0,
        jnp.broadcast_to(log[:, :LINE], (8, LINE)),
        jnp.broadcast_to(log[:, LINE:], (8, LINE)),
    )
    extra = jnp.concatenate([lines, log], axis=0).astype(BF16)
    for dest in range(ROWS):
        for j in range(TC):
            out_ref[dest, :, j * D : (j + 1) * D] = columns[j * TR : (j + 1) * TR, :]
        out_ref[dest, :, TC * D :] = extra
    lane = iota((TR, LINE), 1) - TC * c
    lane1 = iota((1, LINE), 1) - TC * c
    spread = jnp.zeros((TR, LINE), F32)
    trace = jnp.zeros((1, LINE), F32)
    across = horizon_ref[...].T
    for j in range(TC):
        column = jnp.broadcast_to(across[:, j : j + 1], (TR, LINE))
        spread = jnp.where(lane == j, column, spread)
        trace = jnp.where(lane1 == j, trace_ref[j].astype(F32), trace)
    high, low = halves(spread)
    row8 = iota((8, LINE), 0)
    for dest in range(COLS):
        part = jnp.where(row8 == 0, jnp.broadcast_to(trace, (8, LINE)), 0.0)
        part = jnp.where(row8 == 1, jnp.broadcast_to(high[dest : dest + 1], (8, LINE)), part)
        part = jnp.where(row8 == 2, jnp.broadcast_to(low[dest : dest + 1], (8, LINE)), part)
        meta_ref[dest] = part.astype(BF16)
    wide_ref[0:9, :] = conv_ref[...]
    wide_ref[9:10, :] = gain_ref[...]
    wide_ref[10:11, :] = last_ref[...]
    bias = bias_ref[...].T
    rates = [row_ref[...].T / 2048.0, col_ref[...].T / 2048.0]
    for k in range(4):
        side_ref[0, k * HEADS : (k + 1) * HEADS, :] = jnp.broadcast_to(
            bias[:, k : k + 1], (HEADS, LINE)
        )
        side_ref[1, k * HEADS : (k + 1) * HEADS, :] = jnp.broadcast_to(
            rates[k // 2][:, k % 2 : k % 2 + 1], (HEADS, LINE)
        )


def pack_col_kernel(got_ref, own_ref, meta_ref, out_ref, left_ref, right_ref):
    r = lax.axis_index("row")
    up = got_ref[place_of(jnp.maximum(r - 1, 0))].astype(F32)[TR - 1 : TR, :]
    down = got_ref[place_of(jnp.minimum(r + 1, ROWS - 1))].astype(F32)[0:1, :]
    above = jnp.concatenate([up[:, j * D : (j + 1) * D] for j in range(TC)], axis=0)
    below = jnp.concatenate([down[:, j * D : (j + 1) * D] for j in range(TC)], axis=0)
    own = own_ref[...].astype(F32)
    extra = got_ref[:, :, TC * D :].astype(F32)
    logs = jnp.concatenate(
        [
            jnp.concatenate([extra[s, 8 + half : 9 + half, :] for s in ROW_PLACE], axis=0)
            for half in range(2)
        ],
        axis=1,
    )
    rows = [above] + [own[i] for i in range(TR)] + [below]
    rows = [x.astype(BF16) for x in rows]
    logs = logs.astype(BF16)
    for dest, place in enumerate(MID_PLACE):
        for slot in range(3):
            out_ref[place, :, slot * D : (slot + 1) * D] = rows[dest + slot]
        out_ref[place, :, 3 * D : 4 * D] = logs
        out_ref[place, :, 4 * D :] = meta_ref[dest]
    for i, s in enumerate(ROW_PLACE):
        left_ref[i] = got_ref[s, :, 0:D]
        right_ref[i] = got_ref[s, :, (TC - 1) * D : TC * D]


def normalised(hidden, gain):
    scale = lax.rsqrt(jnp.mean(hidden * hidden, axis=-1, keepdims=True) + 1e-06)
    return (hidden * scale * gain).astype(BF16)


def line_scan(cells, tokens, inside, taps, gain, in_w, bc, dt_w, bias, rate, horizon, w_ref, x_ref):
    n = jnp.concatenate([normalised(cells[s] + tokens[s], gain) for s in range(3)], axis=0)
    p = jnp.dot(n, in_w, preferred_element_type=F32).astype(BF16).astype(F32)
    pre = [
        jnp.where(inside[s], p[s * LINE : (s + 1) * LINE, :], 0.0) for s in range(3)
    ]
    shifted = [
        taps[t][0] * pre[0] + taps[t][1] * pre[1] + taps[t][2] * pre[2] for t in range(3)
    ]
    place = iota((LINE, D), 0)
    conv = (
        shifted[1]
        + jnp.where(place == 0, 0.0, pltpu.roll(shifted[0], 1, 0))
        + jnp.where(place == LINE - 1, 0.0, pltpu.roll(shifted[2], LINE - 1, 0))
    )
    mixed = silu(conv).astype(BF16)
    coef = jnp.dot(mixed, bc, preferred_element_type=F32).astype(BF16)
    contract = (((1,), (1,)), ((), ()))
    k = iota((LINE, LINE), 0)
    j = iota((LINE, LINE), 1)
    lower = j <= k
    score_f = lax.dot_general(
        coef[:, STATE : 2 * STATE], coef[:, :STATE], contract, preferred_element_type=F32
    )
    score_b = lax.dot_general(
        coef[:, 3 * STATE :], coef[:, 2 * STATE : 3 * STATE], contract, preferred_element_type=F32
    )
    score_f = jnp.where(lower, score_f, 0.0)
    score_b = jnp.where(j >= k, score_b, 0.0)
    z = lax.dot_general(dt_w, mixed, contract, preferred_element_type=F32) + bias
    step = jnp.maximum(z, 0.0) + jnp.log1p(jnp.exp(-jnp.abs(z)))
    decay = -step * rate - horizon
    high, rest = halves(decay)
    middle, low = halves(rest)
    steps = []
    sums_t = []
    for side in range(2):
        at = slice(side * HEADS, (side + 1) * HEADS)
        steps.append(step[at])
        ones = ((k <= j) if side == 0 else (k >= j)).astype(BF16)
        parts = jnp.concatenate([high[at], middle[at], low[at]], axis=0).astype(BF16)
        total = jnp.dot(parts, ones, preferred_element_type=F32)
        total = total[:HEADS] + (total[HEADS : 2 * HEADS] + total[2 * HEADS :])
        sums_t.append(total)
    sums = [x.T for x in sums_t]
    head_of = iota((LINE, D), 1) // HEAD_DIM
    wide = mixed.astype(F32)
    for h in range(HEADS):
        ahead = sums[0][:, h : h + 1] - sums_t[0][h : h + 1, :]
        behind = sums[1][:, h : h + 1] - sums_t[1][h : h + 1, :]
        decay = jnp.exp(jnp.where(lower, ahead, behind))
        drive = score_f * steps[0][h : h + 1, :] + score_b * steps[1][h : h + 1, :]
        w_ref[:, h * LINE : (h + 1) * LINE] = (drive * decay).astype(BF16)
        x_ref[h * LINE : (h + 1) * LINE, :] = jnp.where(head_of == h, wide, 0.0).astype(BF16)
    return jnp.dot(w_ref[...], x_ref[...], preferred_element_type=F32)


def row_kernel(
    cols_ref,
    wide_ref,
    side_ref,
    cond_ref,
    in_ref,
    bc_ref,
    dt_ref,
    out_ref,
    tokens_ref,
    w_ref,
    x_ref,
):
    r = lax.axis_index("row")
    c = lax.axis_index("col")
    logs, *cells = [
        jnp.stack([cols_ref[p, :, s * D : (s + 1) * D] for p in MID_PLACE])
        .astype(F32)
        .reshape(LINE, D)
        for s in (3, 0, 1, 2)
    ]
    logs = logs.astype(BF16)
    tokens = silu(jnp.dot(logs, cond_ref[...], preferred_element_type=F32)).astype(BF16)
    meta = jnp.sum(cols_ref[:, :, 4 * D :].astype(F32), axis=0)
    trace = jnp.broadcast_to(meta[0:1, :], (8, LINE)).T[:, 0:1].astype(jnp.int32)
    position = iota((1, LINE), 1)
    names = (position & (ROWS - 1)) * COLS + (position >> 3)
    chosen = (names == trace).astype(BF16)
    tokens = jnp.dot(chosen, tokens, preferred_element_type=F32)
    tokens_ref[...] = tokens
    row = r * TR + c
    scanned = line_scan(
        cells,
        [tokens, tokens, tokens],
        [row > 0, True, row < LINE - 1],
        [[wide_ref[3 * s + t : 3 * s + t + 1, :] for s in range(3)] for t in range(3)],
        wide_ref[9:10, :],
        in_ref[:, :D],
        bc_ref[:, : 4 * STATE],
        dt_ref[: 2 * HEADS, :],
        side_ref[0, : 2 * HEADS, :],
        side_ref[1, : 2 * HEADS, :],
        meta[1:2, :] + meta[2:3, :],
        w_ref,
        x_ref,
    )
    out_ref[...] = jnp.concatenate(
        [scanned[i * TC : (i + 1) * TC, :] for i in COL_ORDER], axis=0
    ).astype(BF16)


def column_kernel(
    rows_ref,
    left_ref,
    right_ref,
    tokens_ref,
    own_ref,
    wide_ref,
    side_ref,
    in_ref,
    bc_ref,
    dt_ref,
    hidden_ref,
    gate_ref,
    sum_ref,
    normed_ref,
    pre_ref,
    mixed_ref,
    b_ref,
    cum_ref,
    w_ref,
    y_ref,
):
    r = lax.axis_index("row")
    c = lax.axis_index("col")
    gain = wide_ref[9:10, :]
    hidden = own_ref[...].astype(F32) + tokens_ref[pl.ds(pl.multiple_of(c * TC, TC), TC), :][None]
    hidden = hidden.reshape(LINE, D)
    hidden_ref[...] = hidden
    gate = jnp.dot(normalised(hidden, gain), in_ref[:, D:], preferred_element_type=F32)
    gate_ref[...] = silu(gate.astype(BF16).astype(F32))
    for q in range(TC + 2):
        if q == 0:
            cells = left_ref[...]
        elif q == TC + 1:
            cells = right_ref[...]
        else:
            cells = jnp.stack([rows_ref[s, :, (q - 1) * D : q * D] for s in ROW_PLACE])
        line = jnp.clip(c * TC + q - 1, 0, LINE - 1)
        cells = cells.astype(F32).reshape(LINE, D) + tokens_ref[pl.ds(line, 1), :]
        normed_ref[q * LINE : (q + 1) * LINE, :] = normalised(cells, gain)
    pre_ref[...] = jnp.dot(
        normed_ref[...], in_ref[:, :D], preferred_element_type=F32
    ).astype(BF16)
    place = iota((LINE, D), 0)
    inside = [c > 0] + [True] * TC + [c < COLS - 1]
    for j in range(TC):
        pre = []
        for s in range(3):
            p = pre_ref[(j + s) * LINE : (j + s + 1) * LINE, :].astype(F32)
            pre.append(p if inside[j + s] is True else jnp.where(inside[j + s], p, 0.0))
        shifted = [
            sum(wide_ref[3 * a + s : 3 * a + s + 1, :] * pre[s] for s in range(3))
            for a in range(3)
        ]
        conv = (
            shifted[1]
            + jnp.where(place == 0, 0.0, pltpu.roll(shifted[0], 1, 0))
            + jnp.where(place == LINE - 1, 0.0, pltpu.roll(shifted[2], LINE - 1, 0))
        )
        mixed_ref[j * LINE : (j + 1) * LINE, :] = silu(conv).astype(BF16)
    base = 4 * STATE
    b_weight = jnp.concatenate(
        [bc_ref[:, base : base + STATE], bc_ref[:, base + 2 * STATE : base + 3 * STATE]], axis=1
    )
    c_weight = jnp.concatenate(
        [bc_ref[:, base + STATE : base + 2 * STATE], bc_ref[:, base + 3 * STATE :]], axis=1
    )
    b_ref[...] = jnp.dot(mixed_ref[...], b_weight, preferred_element_type=F32).astype(BF16)
    start = pl.multiple_of(r * TR, TR)
    mine = jnp.concatenate(
        [mixed_ref[pl.ds(j * LINE + start, TR), :] for j in range(TC)], axis=0
    )
    c_own = jnp.dot(mine, c_weight, preferred_element_type=F32)
    ahead_lane = iota((LINE, D), 1) < STATE
    c_ahead = jnp.where(ahead_lane, c_own, 0.0).astype(BF16)
    c_behind = jnp.where(ahead_lane, 0.0, c_own).astype(BF16)
    contract = (((1,), (1,)), ((), ()))
    z = lax.dot_general(
        dt_ref[2 * HEADS :, :], mixed_ref[...], contract, preferred_element_type=F32
    )
    k = iota((LINE, LINE), 0)
    j_ = iota((LINE, LINE), 1)
    extra = rows_ref[:, :, TC * D :].astype(F32)
    owner = iota((TC, LINE), 1) >> 4
    high = jnp.zeros((TC, LINE), F32)
    low = jnp.zeros((TC, LINE), F32)
    for i, s in enumerate(ROW_PLACE):
        high = jnp.where(owner == i, extra[s, :TC, :], high)
        low = jnp.where(owner == (i + ROWS // 2) % ROWS, extra[s, :TC, :], low)
    horizon = high + pltpu.roll(low, LINE // 2, 1)
    steps = []
    sums = []
    for side in range(2):
        bias = side_ref[0, (2 + side) * HEADS : (3 + side) * HEADS, :]
        rate = side_ref[1, (2 + side) * HEADS : (3 + side) * HEADS, :]
        own_steps = []
        decays = []
        for j in range(TC):
            zj = z[side * HEADS : (side + 1) * HEADS, j * LINE : (j + 1) * LINE] + bias
            step = jnp.maximum(zj, 0.0) + jnp.log1p(jnp.exp(-jnp.abs(zj)))
            own_steps.append(step)
            decays.append(-step * rate - horizon[j : j + 1, :])
        decay = jnp.concatenate(decays, axis=0)
        ones = ((k <= j_) if side == 0 else (k >= j_)).astype(BF16)
        high, rest = halves(decay)
        middle, low = halves(rest)
        parts = jnp.concatenate([high, middle, low], axis=0).astype(BF16)
        total = jnp.dot(parts, ones, preferred_element_type=F32)
        total = total[:LINE] + (total[LINE : 2 * LINE] + total[2 * LINE :])
        cum_ref[side] = total.T
        steps.append(own_steps)
        sums.append(total)
    ahead_own = cum_ref[0, pl.ds(start, TR), :]
    behind_own = cum_ref[1, pl.ds(start, TR), :]
    at = iota((TR, LINE), 0) + start
    other = iota((TR, LINE), 1)
    lower = other <= at
    upper = other >= at
    head_of = iota((TR, LINE), 1) >> 4
    for j in range(TC):
        at = slice(j * TR, (j + 1) * TR)
        scores = lax.dot_general(
            jnp.concatenate([c_ahead[at], c_behind[at]], axis=0),
            b_ref[j * LINE : (j + 1) * LINE, :],
            contract,
            preferred_element_type=F32,
        )
        score_f = jnp.where(lower, scores[:TR], 0.0)
        score_b = jnp.where(upper, scores[TR:], 0.0)
        for h in range(HEADS):
            n = j * HEADS + h
            ahead = ahead_own[:, n : n + 1] - sums[0][n : n + 1, :]
            behind = behind_own[:, n : n + 1] - sums[1][n : n + 1, :]
            decay = jnp.exp(jnp.where(lower, ahead, behind))
            drive = score_f * steps[0][j][h : h + 1, :] + score_b * steps[1][j][h : h + 1, :]
            w_ref[j, h * TR : (h + 1) * TR, :] = (drive * decay).astype(BF16)
        for half in range(2):
            at = slice(half * LINE, (half + 1) * LINE)
            full = jnp.dot(
                w_ref[j, at, :],
                mixed_ref[j * LINE : (j + 1) * LINE, at],
                preferred_element_type=F32,
            )
            got = full[:TR, :]
            for h in range(1, HEADS // 2):
                got = jnp.where(head_of == h, full[h * TR : (h + 1) * TR, :], got)
            y_ref[j * TR : (j + 1) * TR, at] = got
    pick = ((k % TC) * TR + k // TC == j_).astype(BF16)
    high, low = halves(y_ref[...])
    sum_ref[...] = jnp.dot(pick, high.astype(BF16), preferred_element_type=F32) + jnp.dot(
        pick, low.astype(BF16), preferred_element_type=F32
    )


def finish_kernel(row_ref, col_ref, hidden_ref, gate_ref, wide_ref, out_w_ref, out_ref):
    by_row = jnp.concatenate([row_ref[s].astype(F32) for s in COL_PLACE], axis=0)
    total = by_row + col_ref[...]
    scale = lax.rsqrt(jnp.mean(total * total, axis=-1, keepdims=True) + 1e-05)
    gated = (total * scale * wide_ref[10:11, :] * gate_ref[...]).astype(BF16)
    branch = jnp.dot(gated, out_w_ref[...], preferred_element_type=F32)
    out_ref[...] = (hidden_ref[...] + branch).reshape(TR, TC, D).astype(BF16)


def call(kernel, outs, *args, scratch=(), smem=0, pinned=True, result=False):
    vmem = pl.BlockSpec(memory_space=pltpu.VMEM)
    specs = [pl.BlockSpec(memory_space=pltpu.SMEM)] * smem + [vmem] * (len(args) - smem)
    if pinned is True:
        pinned = range(smem, len(args))
    args = [
        pltpu.with_memory_space_constraint(x, pltpu.VMEM) if i in pinned else x
        for i, x in enumerate(args)
    ]
    shape = jax.ShapeDtypeStruct if result else pltpu.VMEM
    return pl.pallas_call(
        kernel,
        out_shape=[shape(s, d) for s, d in outs],
        in_specs=specs,
        out_specs=[vmem] * len(outs),
        scratch_shapes=list(scratch),
        name=kernel.__name__,
    )(*args)


def per_device(
    latent,
    well_logs,
    cond_weight,
    trace_rows,
    norm_gain,
    in_weight,
    conv_weight,
    bc_weight,
    dt_weight,
    dt_bias,
    row_rate,
    col_rate,
    horizon,
    out_gain,
    out_weight,
):
    dt_weight = dt_weight.T
    packed, meta, own, wide, side = call(
        pack_row_kernel,
        [
            ((ROWS, TR, TC * D + LINE), BF16),
            ((COLS, 8, LINE), BF16),
            ((TR, TC, D), BF16),
            ((16, D), F32),
            ((2, 4 * HEADS, LINE), F32),
        ],
        trace_rows,
        latent,
        well_logs,
        horizon.T,
        norm_gain.reshape(1, D),
        out_gain.reshape(1, D),
        conv_weight,
        dt_bias,
        row_rate,
        col_rate,
        smem=1,
        pinned=(),
    )
    from_rows = lax.all_to_all(
        packed, "row", 0, 0, tiled=True, axis_index_groups=[list(ROW_ORDER)]
    )
    packed, first, last = call(
        pack_col_kernel,
        [((COLS, 8, 4 * D + LINE), BF16), ((ROWS, TR, D), BF16), ((ROWS, TR, D), BF16)],
        from_rows,
        own,
        meta,
    )
    ends = COLS - 1
    right = lax.ppermute(first, "col", [(i + 1, i) for i in range(ends)])
    left = lax.ppermute(last, "col", [(i, i + 1) for i in range(ends)])
    from_cols = lax.all_to_all(
        packed, "col", 0, 0, tiled=True, axis_index_groups=[list(MID_ORDER)]
    )
    by_row, tokens = call(
        row_kernel,
        [((LINE, D), BF16), ((LINE, D), F32)],
        from_cols,
        wide,
        side,
        cond_weight,
        in_weight,
        bc_weight,
        dt_weight,
        scratch=[
            pltpu.VMEM((LINE, HEADS * LINE), BF16),
            pltpu.VMEM((HEADS * LINE, D), BF16),
        ],
    )
    by_row = lax.all_to_all(
        by_row.reshape(COLS, TC, D), "col", 0, 0, tiled=True, axis_index_groups=[list(COL_ORDER)]
    )
    hidden, gate, by_column = call(
        column_kernel,
        [((LINE, D), F32), ((LINE, D), F32), ((LINE, D), F32)],
        from_rows,
        left,
        right,
        tokens,
        own,
        wide,
        side,
        in_weight,
        bc_weight,
        dt_weight,
        scratch=[
            pltpu.VMEM(((TC + 2) * LINE, D), BF16),
            pltpu.VMEM(((TC + 2) * LINE, D), BF16),
            pltpu.VMEM((TC * LINE, D), BF16),
            pltpu.VMEM((TC * LINE, 2 * STATE), BF16),
            pltpu.VMEM((2, LINE, LINE), F32),
            pltpu.VMEM((TC, HEADS * TR, LINE), BF16),
            pltpu.VMEM((LINE, D), F32),
        ],
    )
    (out,) = call(
        finish_kernel,
        [((TR, TC, D), BF16)],
        by_row,
        by_column,
        hidden,
        gate,
        wide,
        out_weight,
        result=True,
    )
    return out


def solution(mesh):
    placed = (
        P("row", "col", None),
        P(("row", "col"), None),
        P(),
        P("col"),
        P(),
        P(),
        P(),
        P(),
        P(),
        P(),
        P(),
        P(),
        P("row", "col"),
        P(),
        P(),
    )
    return jax.shard_map(
        per_device, mesh=mesh, in_specs=placed, out_specs=P("row", "col", None), check_vma=False
    )
```

```python
import jax
import jax.numpy as jnp
from jax import lax
from jax.experimental import pallas as pl
from jax.experimental.pallas import tpu as pltpu
from jax.sharding import PartitionSpec as P

F32 = jnp.float32
BF16 = jnp.bfloat16
ROWS = 8
COLS = 16
TR = 16
TC = 8
LINE = 128
D = 256
HEADS = 16
HEAD_DIM = 16
STATE = 128
ROW_ORDER = (5, 7, 3, 1, 4, 6, 2, 0)
COL_ORDER = (15, 14, 13, 12, 11, 10, 9, 8, 7, 6, 5, 4, 3, 2, 1, 0)
ROW_PLACE = tuple(ROW_ORDER.index(i) for i in range(ROWS))
MID_ORDER = (15, 14, 13, 12, 11, 10, 9, 8, 7, 6, 5, 4, 3, 2, 1, 0)
MID_PLACE = tuple(MID_ORDER.index(i) for i in range(COLS))
COL_PLACE = tuple(COL_ORDER.index(i) for i in range(COLS))


def iota(shape, dim):
    return lax.broadcasted_iota(jnp.int32, shape, dim)


def place_of(row):
    return sum(jnp.where(row == i, ROW_PLACE[i], 0) for i in range(ROWS))


def halves(x):
    high = x.astype(BF16).astype(F32)
    return high, x - high


def silu(x):
    return x * jax.nn.sigmoid(x)


def pack_row_kernel(
    trace_ref,
    latent_ref,
    logs_ref,
    horizon_ref,
    gain_ref,
    last_ref,
    conv_ref,
    bias_ref,
    row_ref,
    col_ref,
    out_ref,
    meta_ref,
    own_ref,
    wide_ref,
    side_ref,
):
    r = lax.axis_index("row")
    c = lax.axis_index("col")
    own_ref[...] = latent_ref[...]
    target = iota((LINE, LINE), 0)
    source = iota((LINE, LINE), 1)
    pick = ((target & (TR - 1)) * TC + (target >> 4) == source).astype(BF16)
    flat = latent_ref[...].astype(F32).reshape(LINE, D).astype(BF16)
    columns = jnp.dot(pick, flat, preferred_element_type=F32).astype(BF16)
    high, low = halves(horizon_ref[...])
    place = iota((TR, LINE), 1)
    cell = iota((TR, LINE), 0)
    first = (place - TR * r == cell).astype(BF16)
    second = (place - ((TR * r + LINE // 2) & (LINE - 1)) == cell).astype(BF16)
    lines = jnp.dot(high.astype(BF16), first, preferred_element_type=F32) + jnp.dot(
        low.astype(BF16), second, preferred_element_type=F32
    )
    log = logs_ref[...].astype(F32)
    row8 = iota((8, LINE), 0)
    log = jnp.where(
        row8 == 0,
        jnp.broadcast_to(log[:, :LINE], (8, LINE)),
        jnp.broadcast_to(log[:, LINE:], (8, LINE)),
    )
    extra = jnp.concatenate([lines, log], axis=0).astype(BF16)
    for dest in range(ROWS):
        for j in range(TC):
            out_ref[dest, :, j * D : (j + 1) * D] = columns[j * TR : (j + 1) * TR, :]
        out_ref[dest, :, TC * D :] = extra
    lane = iota((TR, LINE), 1) - TC * c
    lane1 = iota((1, LINE), 1) - TC * c
    spread = jnp.zeros((TR, LINE), F32)
    trace = jnp.zeros((1, LINE), F32)
    across = horizon_ref[...].T
    for j in range(TC):
        column = jnp.broadcast_to(across[:, j : j + 1], (TR, LINE))
        spread = jnp.where(lane == j, column, spread)
        trace = jnp.where(lane1 == j, trace_ref[j].astype(F32), trace)
    high, low = halves(spread)
    row8 = iota((8, LINE), 0)
    for dest in range(COLS):
        part = jnp.where(row8 == 0, jnp.broadcast_to(trace, (8, LINE)), 0.0)
        part = jnp.where(row8 == 1, jnp.broadcast_to(high[dest : dest + 1], (8, LINE)), part)
        part = jnp.where(row8 == 2, jnp.broadcast_to(low[dest : dest + 1], (8, LINE)), part)
        meta_ref[dest] = part.astype(BF16)
    wide_ref[0:9, :] = conv_ref[...]
    wide_ref[9:10, :] = gain_ref[...]
    wide_ref[10:11, :] = last_ref[...]
    bias = bias_ref[...].T
    rates = [row_ref[...].T / 2048.0, col_ref[...].T / 2048.0]
    for k in range(4):
        side_ref[0, k * HEADS : (k + 1) * HEADS, :] = jnp.broadcast_to(
            bias[:, k : k + 1], (HEADS, LINE)
        )
        side_ref[1, k * HEADS : (k + 1) * HEADS, :] = jnp.broadcast_to(
            rates[k // 2][:, k % 2 : k % 2 + 1], (HEADS, LINE)
        )


def pack_col_kernel(got_ref, own_ref, meta_ref, out_ref, near_ref, far_ref):
    r = lax.axis_index("row")
    even = (lax.axis_index("col") & 1) == 0
    up = got_ref[place_of(jnp.maximum(r - 1, 0))].astype(F32)[TR - 1 : TR, :]
    down = got_ref[place_of(jnp.minimum(r + 1, ROWS - 1))].astype(F32)[0:1, :]
    above = jnp.concatenate([up[:, j * D : (j + 1) * D] for j in range(TC)], axis=0)
    below = jnp.concatenate([down[:, j * D : (j + 1) * D] for j in range(TC)], axis=0)
    own = own_ref[...].astype(F32)
    extra = got_ref[:, :, TC * D :].astype(F32)
    logs = jnp.concatenate(
        [
            jnp.concatenate([extra[s, 8 + half : 9 + half, :] for s in ROW_PLACE], axis=0)
            for half in range(2)
        ],
        axis=1,
    )
    rows = [above] + [own[i] for i in range(TR)] + [below]
    rows = [x.astype(BF16) for x in rows]
    logs = logs.astype(BF16)
    for dest, place in enumerate(MID_PLACE):
        for slot in range(3):
            out_ref[place, :, slot * D : (slot + 1) * D] = rows[dest + slot]
        out_ref[place, :, 3 * D : 4 * D] = logs
        out_ref[place, :, 4 * D :] = meta_ref[dest]
    for i, s in enumerate(ROW_PLACE):
        first = got_ref[s, :, 0:D]
        last = got_ref[s, :, (TC - 1) * D : TC * D]
        near_ref[i] = jnp.where(even, last, first)
        far_ref[i] = jnp.where(even, first, last)


def normalised(hidden, gain):
    scale = lax.rsqrt(jnp.mean(hidden * hidden, axis=-1, keepdims=True) + 1e-06)
    return (hidden * scale * gain).astype(BF16)


def line_scan(cells, tokens, inside, taps, gain, in_w, bc, dt_w, bias, rate, horizon, w_ref, x_ref):
    n = jnp.concatenate([normalised(cells[s] + tokens[s], gain) for s in range(3)], axis=0)
    p = jnp.dot(n, in_w, preferred_element_type=F32).astype(BF16).astype(F32)
    pre = [
        jnp.where(inside[s], p[s * LINE : (s + 1) * LINE, :], 0.0) for s in range(3)
    ]
    shifted = [
        taps[t][0] * pre[0] + taps[t][1] * pre[1] + taps[t][2] * pre[2] for t in range(3)
    ]
    place = iota((LINE, D), 0)
    conv = (
        shifted[1]
        + jnp.where(place == 0, 0.0, pltpu.roll(shifted[0], 1, 0))
        + jnp.where(place == LINE - 1, 0.0, pltpu.roll(shifted[2], LINE - 1, 0))
    )
    mixed = silu(conv).astype(BF16)
    coef = jnp.dot(mixed, bc, preferred_element_type=F32).astype(BF16)
    contract = (((1,), (1,)), ((), ()))
    k = iota((LINE, LINE), 0)
    j = iota((LINE, LINE), 1)
    lower = j <= k
    score_f = lax.dot_general(
        coef[:, STATE : 2 * STATE], coef[:, :STATE], contract, preferred_element_type=F32
    )
    score_b = lax.dot_general(
        coef[:, 3 * STATE :], coef[:, 2 * STATE : 3 * STATE], contract, preferred_element_type=F32
    )
    score_f = jnp.where(lower, score_f, 0.0)
    score_b = jnp.where(j >= k, score_b, 0.0)
    z = lax.dot_general(dt_w, mixed, contract, preferred_element_type=F32) + bias
    step = jnp.maximum(z, 0.0) + jnp.log1p(jnp.exp(-jnp.abs(z)))
    decay = -step * rate - horizon
    high, rest = halves(decay)
    middle, low = halves(rest)
    steps = []
    sums_t = []
    for side in range(2):
        at = slice(side * HEADS, (side + 1) * HEADS)
        steps.append(step[at])
        ones = ((k <= j) if side == 0 else (k >= j)).astype(BF16)
        parts = jnp.concatenate([high[at], middle[at], low[at]], axis=0).astype(BF16)
        total = jnp.dot(parts, ones, preferred_element_type=F32)
        total = total[:HEADS] + (total[HEADS : 2 * HEADS] + total[2 * HEADS :])
        sums_t.append(total)
    sums = [x.T for x in sums_t]
    head_of = iota((LINE, D), 1) // HEAD_DIM
    wide = mixed.astype(F32)
    for h in range(HEADS):
        ahead = sums[0][:, h : h + 1] - sums_t[0][h : h + 1, :]
        behind = sums[1][:, h : h + 1] - sums_t[1][h : h + 1, :]
        decay = jnp.exp(jnp.where(lower, ahead, behind))
        drive = score_f * steps[0][h : h + 1, :] + score_b * steps[1][h : h + 1, :]
        w_ref[:, h * LINE : (h + 1) * LINE] = (drive * decay).astype(BF16)
        x_ref[h * LINE : (h + 1) * LINE, :] = jnp.where(head_of == h, wide, 0.0).astype(BF16)
    return jnp.dot(w_ref[...], x_ref[...], preferred_element_type=F32)


def row_kernel(
    cols_ref,
    wide_ref,
    side_ref,
    cond_ref,
    in_ref,
    bc_ref,
    dt_ref,
    out_ref,
    tokens_ref,
    w_ref,
    x_ref,
):
    r = lax.axis_index("row")
    c = lax.axis_index("col")
    logs, *cells = [
        jnp.stack([cols_ref[p, :, s * D : (s + 1) * D] for p in MID_PLACE])
        .astype(F32)
        .reshape(LINE, D)
        for s in (3, 0, 1, 2)
    ]
    logs = logs.astype(BF16)
    tokens = silu(jnp.dot(logs, cond_ref[...], preferred_element_type=F32)).astype(BF16)
    meta = jnp.sum(cols_ref[:, :, 4 * D :].astype(F32), axis=0)
    trace = jnp.broadcast_to(meta[0:1, :], (8, LINE)).T[:, 0:1].astype(jnp.int32)
    position = iota((1, LINE), 1)
    names = (position & (ROWS - 1)) * COLS + (position >> 3)
    chosen = (names == trace).astype(BF16)
    tokens = jnp.dot(chosen, tokens, preferred_element_type=F32)
    tokens_ref[...] = tokens
    row = r * TR + c
    scanned = line_scan(
        cells,
        [tokens, tokens, tokens],
        [row > 0, True, row < LINE - 1],
        [[wide_ref[3 * s + t : 3 * s + t + 1, :] for s in range(3)] for t in range(3)],
        wide_ref[9:10, :],
        in_ref[:, :D],
        bc_ref[:, : 4 * STATE],
        dt_ref[: 2 * HEADS, :],
        side_ref[0, : 2 * HEADS, :],
        side_ref[1, : 2 * HEADS, :],
        meta[1:2, :] + meta[2:3, :],
        w_ref,
        x_ref,
    )
    out_ref[...] = jnp.concatenate(
        [scanned[i * TC : (i + 1) * TC, :] for i in COL_ORDER], axis=0
    ).astype(BF16)


def column_kernel(
    rows_ref,
    near_ref,
    far_ref,
    tokens_ref,
    own_ref,
    wide_ref,
    side_ref,
    in_ref,
    bc_ref,
    dt_ref,
    hidden_ref,
    gate_ref,
    sum_ref,
    normed_ref,
    pre_ref,
    mixed_ref,
    b_ref,
    cum_ref,
    w_ref,
    y_ref,
):
    r = lax.axis_index("row")
    c = lax.axis_index("col")
    gain = wide_ref[9:10, :]
    hidden = own_ref[...].astype(F32) + tokens_ref[pl.ds(pl.multiple_of(c * TC, TC), TC), :][None]
    hidden = hidden.reshape(LINE, D)
    hidden_ref[...] = hidden
    gate = jnp.dot(normalised(hidden, gain), in_ref[:, D:], preferred_element_type=F32)
    gate_ref[...] = silu(gate.astype(BF16).astype(F32))
    for q in range(TC + 2):
        if q == 0:
            cells = jnp.where((c & 1) == 0, far_ref[...], near_ref[...])
        elif q == TC + 1:
            cells = jnp.where((c & 1) == 0, near_ref[...], far_ref[...])
        else:
            cells = jnp.stack([rows_ref[s, :, (q - 1) * D : q * D] for s in ROW_PLACE])
        line = jnp.clip(c * TC + q - 1, 0, LINE - 1)
        cells = cells.astype(F32).reshape(LINE, D) + tokens_ref[pl.ds(line, 1), :]
        normed_ref[q * LINE : (q + 1) * LINE, :] = normalised(cells, gain)
    pre_ref[...] = jnp.dot(
        normed_ref[...], in_ref[:, :D], preferred_element_type=F32
    ).astype(BF16)
    place = iota((LINE, D), 0)
    inside = [c > 0] + [True] * TC + [c < COLS - 1]
    for j in range(TC):
        pre = []
        for s in range(3):
            p = pre_ref[(j + s) * LINE : (j + s + 1) * LINE, :].astype(F32)
            pre.append(p if inside[j + s] is True else jnp.where(inside[j + s], p, 0.0))
        shifted = [
            sum(wide_ref[3 * a + s : 3 * a + s + 1, :] * pre[s] for s in range(3))
            for a in range(3)
        ]
        conv = (
            shifted[1]
            + jnp.where(place == 0, 0.0, pltpu.roll(shifted[0], 1, 0))
            + jnp.where(place == LINE - 1, 0.0, pltpu.roll(shifted[2], LINE - 1, 0))
        )
        mixed_ref[j * LINE : (j + 1) * LINE, :] = silu(conv).astype(BF16)
    base = 4 * STATE
    b_weight = jnp.concatenate(
        [bc_ref[:, base : base + STATE], bc_ref[:, base + 2 * STATE : base + 3 * STATE]], axis=1
    )
    c_weight = jnp.concatenate(
        [bc_ref[:, base + STATE : base + 2 * STATE], bc_ref[:, base + 3 * STATE :]], axis=1
    )
    b_ref[...] = jnp.dot(mixed_ref[...], b_weight, preferred_element_type=F32).astype(BF16)
    start = pl.multiple_of(r * TR, TR)
    mine = jnp.concatenate(
        [mixed_ref[pl.ds(j * LINE + start, TR), :] for j in range(TC)], axis=0
    )
    c_own = jnp.dot(mine, c_weight, preferred_element_type=F32)
    ahead_lane = iota((LINE, D), 1) < STATE
    c_ahead = jnp.where(ahead_lane, c_own, 0.0).astype(BF16)
    c_behind = jnp.where(ahead_lane, 0.0, c_own).astype(BF16)
    contract = (((1,), (1,)), ((), ()))
    z = lax.dot_general(
        dt_ref[2 * HEADS :, :], mixed_ref[...], contract, preferred_element_type=F32
    )
    k = iota((LINE, LINE), 0)
    j_ = iota((LINE, LINE), 1)
    extra = rows_ref[:, :, TC * D :].astype(F32)
    owner = iota((TC, LINE), 1) >> 4
    high = jnp.zeros((TC, LINE), F32)
    low = jnp.zeros((TC, LINE), F32)
    for i, s in enumerate(ROW_PLACE):
        high = jnp.where(owner == i, extra[s, :TC, :], high)
        low = jnp.where(owner == (i + ROWS // 2) % ROWS, extra[s, :TC, :], low)
    horizon = high + pltpu.roll(low, LINE // 2, 1)
    steps = []
    sums = []
    for side in range(2):
        bias = side_ref[0, (2 + side) * HEADS : (3 + side) * HEADS, :]
        rate = side_ref[1, (2 + side) * HEADS : (3 + side) * HEADS, :]
        own_steps = []
        decays = []
        for j in range(TC):
            zj = z[side * HEADS : (side + 1) * HEADS, j * LINE : (j + 1) * LINE] + bias
            step = jnp.maximum(zj, 0.0) + jnp.log1p(jnp.exp(-jnp.abs(zj)))
            own_steps.append(step)
            decays.append(-step * rate - horizon[j : j + 1, :])
        decay = jnp.concatenate(decays, axis=0)
        ones = ((k <= j_) if side == 0 else (k >= j_)).astype(BF16)
        high, rest = halves(decay)
        middle, low = halves(rest)
        parts = jnp.concatenate([high, middle, low], axis=0).astype(BF16)
        total = jnp.dot(parts, ones, preferred_element_type=F32)
        total = total[:LINE] + (total[LINE : 2 * LINE] + total[2 * LINE :])
        cum_ref[side] = total.T
        steps.append(own_steps)
        sums.append(total)
    ahead_own = cum_ref[0, pl.ds(start, TR), :]
    behind_own = cum_ref[1, pl.ds(start, TR), :]
    at = iota((TR, LINE), 0) + start
    other = iota((TR, LINE), 1)
    lower = other <= at
    upper = other >= at
    head_of = iota((TR, LINE), 1) >> 4
    for j in range(TC):
        at = slice(j * TR, (j + 1) * TR)
        scores = lax.dot_general(
            jnp.concatenate([c_ahead[at], c_behind[at]], axis=0),
            b_ref[j * LINE : (j + 1) * LINE, :],
            contract,
            preferred_element_type=F32,
        )
        score_f = jnp.where(lower, scores[:TR], 0.0)
        score_b = jnp.where(upper, scores[TR:], 0.0)
        for h in range(HEADS):
            n = j * HEADS + h
            ahead = ahead_own[:, n : n + 1] - sums[0][n : n + 1, :]
            behind = behind_own[:, n : n + 1] - sums[1][n : n + 1, :]
            decay = jnp.exp(jnp.where(lower, ahead, behind))
            drive = score_f * steps[0][j][h : h + 1, :] + score_b * steps[1][j][h : h + 1, :]
            w_ref[j, h * TR : (h + 1) * TR, :] = (drive * decay).astype(BF16)
        for half in range(2):
            at = slice(half * LINE, (half + 1) * LINE)
            full = jnp.dot(
                w_ref[j, at, :],
                mixed_ref[j * LINE : (j + 1) * LINE, at],
                preferred_element_type=F32,
            )
            got = full[:TR, :]
            for h in range(1, HEADS // 2):
                got = jnp.where(head_of == h, full[h * TR : (h + 1) * TR, :], got)
            y_ref[j * TR : (j + 1) * TR, at] = got
    pick = ((k % TC) * TR + k // TC == j_).astype(BF16)
    high, low = halves(y_ref[...])
    sum_ref[...] = jnp.dot(pick, high.astype(BF16), preferred_element_type=F32) + jnp.dot(
        pick, low.astype(BF16), preferred_element_type=F32
    )


def finish_kernel(row_ref, col_ref, hidden_ref, gate_ref, wide_ref, out_w_ref, out_ref):
    by_row = jnp.concatenate([row_ref[s].astype(F32) for s in COL_PLACE], axis=0)
    total = by_row + col_ref[...]
    scale = lax.rsqrt(jnp.mean(total * total, axis=-1, keepdims=True) + 1e-05)
    gated = (total * scale * wide_ref[10:11, :] * gate_ref[...]).astype(BF16)
    branch = jnp.dot(gated, out_w_ref[...], preferred_element_type=F32)
    out_ref[...] = (hidden_ref[...] + branch).reshape(TR, TC, D).astype(BF16)


def call(kernel, outs, *args, scratch=(), smem=0, pinned=True, result=False):
    vmem = pl.BlockSpec(memory_space=pltpu.VMEM)
    specs = [pl.BlockSpec(memory_space=pltpu.SMEM)] * smem + [vmem] * (len(args) - smem)
    if pinned is True:
        pinned = range(smem, len(args))
    args = [
        pltpu.with_memory_space_constraint(x, pltpu.VMEM) if i in pinned else x
        for i, x in enumerate(args)
    ]
    shape = jax.ShapeDtypeStruct if result else pltpu.VMEM
    return pl.pallas_call(
        kernel,
        out_shape=[shape(s, d) for s, d in outs],
        in_specs=specs,
        out_specs=[vmem] * len(outs),
        scratch_shapes=list(scratch),
        name=kernel.__name__,
    )(*args)


def per_device(
    latent,
    well_logs,
    cond_weight,
    trace_rows,
    norm_gain,
    in_weight,
    conv_weight,
    bc_weight,
    dt_weight,
    dt_bias,
    row_rate,
    col_rate,
    horizon,
    out_gain,
    out_weight,
):
    dt_weight = dt_weight.T
    packed, meta, own, wide, side = call(
        pack_row_kernel,
        [
            ((ROWS, TR, TC * D + LINE), BF16),
            ((COLS, 8, LINE), BF16),
            ((TR, TC, D), BF16),
            ((16, D), F32),
            ((2, 4 * HEADS, LINE), F32),
        ],
        trace_rows,
        latent,
        well_logs,
        horizon.T,
        norm_gain.reshape(1, D),
        out_gain.reshape(1, D),
        conv_weight,
        dt_bias,
        row_rate,
        col_rate,
        smem=1,
        pinned=(),
    )
    from_rows = lax.all_to_all(
        packed, "row", 0, 0, tiled=True, axis_index_groups=[list(ROW_ORDER)]
    )
    packed, near, far = call(
        pack_col_kernel,
        [((COLS, 8, 4 * D + LINE), BF16), ((ROWS, TR, D), BF16), ((ROWS, TR, D), BF16)],
        from_rows,
        own,
        meta,
    )
    near = lax.ppermute(near, "col", [(i, i ^ 1) for i in range(COLS)])
    pairs = [(i, i + 1) for i in range(1, COLS - 1, 2)]
    far = lax.ppermute(far, "col", pairs + [(j, i) for i, j in pairs])
    from_cols = lax.all_to_all(
        packed, "col", 0, 0, tiled=True, axis_index_groups=[list(MID_ORDER)]
    )
    by_row, tokens = call(
        row_kernel,
        [((LINE, D), BF16), ((LINE, D), F32)],
        from_cols,
        wide,
        side,
        cond_weight,
        in_weight,
        bc_weight,
        dt_weight,
        scratch=[
            pltpu.VMEM((LINE, HEADS * LINE), BF16),
            pltpu.VMEM((HEADS * LINE, D), BF16),
        ],
    )
    by_row = lax.all_to_all(
        by_row.reshape(COLS, TC, D), "col", 0, 0, tiled=True, axis_index_groups=[list(COL_ORDER)]
    )
    hidden, gate, by_column = call(
        column_kernel,
        [((LINE, D), F32), ((LINE, D), F32), ((LINE, D), F32)],
        from_rows,
        near,
        far,
        tokens,
        own,
        wide,
        side,
        in_weight,
        bc_weight,
        dt_weight,
        scratch=[
            pltpu.VMEM(((TC + 2) * LINE, D), BF16),
            pltpu.VMEM(((TC + 2) * LINE, D), BF16),
            pltpu.VMEM((TC * LINE, D), BF16),
            pltpu.VMEM((TC * LINE, 2 * STATE), BF16),
            pltpu.VMEM((2, LINE, LINE), F32),
            pltpu.VMEM((TC, HEADS * TR, LINE), BF16),
            pltpu.VMEM((LINE, D), F32),
        ],
    )
    (out,) = call(
        finish_kernel,
        [((TR, TC, D), BF16)],
        by_row,
        by_column,
        hidden,
        gate,
        wide,
        out_weight,
        result=True,
    )
    return out


def solution(mesh):
    placed = (
        P("row", "col", None),
        P(("row", "col"), None),
        P(),
        P("col"),
        P(),
        P(),
        P(),
        P(),
        P(),
        P(),
        P(),
        P(),
        P("row", "col"),
        P(),
        P(),
    )
    return jax.shard_map(
        per_device, mesh=mesh, in_specs=placed, out_specs=P("row", "col", None), check_vma=False
    )
```
